256 devices in a mesh: rows: 32 (over z, y), cols: 8 (over x, core).
Axes of the slice: x: 4, y: 4, z: 8, core: 2. Of those that a mesh axis runs over, the one named last changes fastest.
Arguments:
- features: float32 [32768, 4, 8, 256], P('rows', None, 'cols'), may hold values from -6 to 6
Outputs:
- factor_rows: float32 [512, 4, 8, 256], P(None, None, 'cols')
- basis: float32 [32768, 2, 256], P('rows')
- trailing: float32 [32768, 4, 8, 256], P('rows', None, 'cols')
The draws below stay inside these ranges and needn't reach their ends.
All inputs are finite; a program needn't handle non-finite values.
Results may differ from the reference program's by a relative error of at most 0.0003.
Values sent between devices are 32-bit elements; how exact they have to be, the bound alone decides.
A program may use at most 64 MiB of HBM per device.

```python
import math
import jax
import jax.numpy as jnp
from jax import lax

PW = 256
PAN_DEV = 4
ROWS = 32768
N_COLS = 8


def draw_features(key, part):
    subkeys = jax.random.split(key, 4)
    full_shape = (ROWS, PAN_DEV, N_COLS, PW)
    row_shape = (ROWS, PAN_DEV, N_COLS, 1)
    column_shape = (1, PAN_DEV, N_COLS, PW)
    position = jnp.arange(ROWS, dtype=jnp.float32).reshape(ROWS, 1, 1, 1) / (ROWS - 1.0)
    noise = jnp.clip(jax.random.normal(subkeys[0], full_shape, jnp.float32), -4.0, 4.0)
    common = jnp.clip(jax.random.normal(subkeys[1], row_shape, jnp.float32), -4.0, 4.0)
    rising = jnp.exp(position * math.log(3.0)) * 0.6
    loading = jax.random.uniform(subkeys[2], column_shape, jnp.float32, 0.2, 0.6)
    spread = jax.random.uniform(subkeys[3], column_shape, jnp.float32, 0.5, 1.5)
    return jnp.clip(rising * (loading * common + spread * noise), -6.0, 6.0)


def setup_inputs(seed: int = 0) -> dict:
    streams_of = jax.random.split(jax.random.key(seed), 2)
    features = draw_features(jax.random.fold_in(streams_of[1], 71), 0)
    return dict(features=features)


def orthonormal(panel):
    qmat, rmat = jnp.linalg.qr(panel)
    signs = jnp.sign(jnp.diagonal(rmat))
    return qmat * signs[None, :]

def reference(features):
    matrix = features.reshape(ROWS, PAN_DEV * N_COLS * PW)
    basis_a = orthonormal(matrix[:, :PW])
    proj_a = jnp.dot(basis_a.T, matrix, precision=lax.Precision.HIGHEST)
    updated = matrix - jnp.dot(basis_a, proj_a, precision=lax.Precision.HIGHEST)
    basis_b = orthonormal(updated[:, PW:2 * PW])
    proj_b = jnp.dot(basis_b.T, updated, precision=lax.Precision.HIGHEST)
    final = updated - jnp.dot(basis_b, proj_b, precision=lax.Precision.HIGHEST)
    factor_rows = jnp.concatenate([proj_a, proj_b], axis=0).reshape(2 * PW, PAN_DEV, N_COLS, PW)
    basis = jnp.stack([basis_a, basis_b], axis=1)
    return (factor_rows, basis, final.reshape(ROWS, PAN_DEV, N_COLS, PW))
```

```python
import jax
import jax.numpy as jnp
from jax import lax
from jax.experimental import pallas as pl
from jax.experimental.pallas import tpu as pltpu
from jax.sharding import PartitionSpec as P

HIGHEST = lax.Precision.HIGHEST
F32 = jnp.float32
BF16 = jnp.bfloat16
MESH = pl.DeviceIdType.MESH

NY = 4
NZ = 8
NX = 4
ROWS = 1024
WIDTH = 512
B = 128
GR = 8
TILES = 8
TY = 6
CH = 128
NCH = ROWS // CH


def dot(a, b, dims):
    return lax.dot_general(a, b, (dims, ((), ())), precision=HIGHEST, preferred_element_type=F32)


def split(value):
    high = value.astype(BF16)
    return high, (value - high.astype(F32)).astype(BF16)


def dot3(a, b, dims):
    def one(u, v):
        return lax.dot_general(u, v, (dims, ((), ())), preferred_element_type=F32)

    return one(a[0], b[0]) + (one(a[0], b[1]) + one(a[1], b[0]))

def rows_bcast(x, j):
    return jnp.broadcast_to(x[j:j + 1, :], x.shape)

def lane_bcast(x, c):
    return jnp.broadcast_to(x[:, c:c + 1], x.shape)

def leaf(x_ref):
    n = B // GR
    lane = lax.broadcasted_iota(jnp.int32, (GR, B), 1)
    sub = lax.broadcasted_iota(jnp.int32, (GR, B), 0)
    x = [x_ref[GR * t:GR * (t + 1), :] for t in range(n)]
    for g in range(n):
        base = GR * g
        cur = x[g]
        v = [lane_bcast(cur, base + c) for c in range(GR)]
        in_group = (lane >= base) & (lane < base + GR)
        scale, mult, rows = [], {}, []
        for j in range(GR):
            r = lax.rsqrt(rows_bcast(v[j], j))
            w = jnp.where(sub > j, v[j] * r, 0.0)
            row = jnp.where(lane == base + j, r, rows_bcast(cur, j) * r)
            cur = jnp.where(sub == j, row, jnp.where((lane == base + j) & (sub > j), 0.0, cur) - w * row)
            for c in range(j + 1, GR):
                m = rows_bcast(v[c], j) * r
                mult[j, c] = m
                v[c] = v[c] - w * m
            scale.append(r)
            rows.append(jnp.where(in_group & (lane > base + j), 0.0, row))
        x[g] = cur
        for t in range(g + 1, n):
            xt = x[t]
            u = [lane_bcast(xt, base + c) for c in range(GR)]
            xt = jnp.where(in_group, 0.0, xt)
            for j in range(GR):
                w = u[j] * scale[j]
                for c in range(j + 1, GR):
                    u[c] = u[c] - w * mult[j, c]
                xt = xt - w * rows[j]
            x[t] = xt
    for t in range(n):
        x_ref[GR * t:GR * (t + 1), :] = x[t]

def chol_inv(x_ref, d_ref):
    size = x_ref.shape[0]
    nb = size // B
    for k in range(nb):
        sl = slice(B * k, B * (k + 1))
        d_ref[...] = x_ref[sl, sl]
        leaf(d_ref)
        ri = lax.broadcasted_iota(jnp.int32, (B, B), 0)
        ci = lax.broadcasted_iota(jnp.int32, (B, B), 1)
        m = jnp.where(ri >= ci, d_ref[...], 0.0)
        x_ref[sl, sl] = m
        if k:
            left = dot(m, x_ref[sl, :B * k], ((1,), (0,)))
            x_ref[sl, :B * k] = left
        if k < nb - 1:
            hi = slice(B * (k + 1), size)
            up = dot(m, x_ref[sl, hi], ((1,), (0,)))
            x_ref[sl, hi] = jnp.zeros_like(up)
            lo = slice(B * (k + 1), size)
            x_ref[lo, hi] = x_ref[lo, hi] - dot(up, up, ((0,), (0,)))
            x_ref[lo, sl] = -dot(up, m, ((0,), (0,)))
            if k:
                x_ref[lo, :B * k] = x_ref[lo, :B * k] - dot(up, left, ((0,), (0,)))


def each(count, body):
    def step(i, carry):
        body(i + 1)
        return carry

    lax.fori_loop(0, count, step, 0)


def exchange(count, make):
    each(count, lambda d: make(d).start())


def arrived(count, make):
    each(count, lambda d: make(d).wait_recv())


def sent(count, make):
    each(count, lambda d: make(d).wait_send())


def gather_kernel(
    a_hbm, p_hbm, gram_hbm, g_hbm,
    av, pt, gs, gy, gsum, gz, gram, gl, gf, ry, sy, rz2, rz1, sz, ry2,
    load_sem, ring_s, ring_r, core_s, core_r, gy_s, gy_r, gz_s, gz_r, ga_s, ga_r, gx_s, gx_r, gc_s, gc_r,
    y1_s, y1_r, z1_s, z1_r, z2_s, z2_r, y2_s, y2_r, z3_s, z3_r, y3_s, y3_r, y4_s, y4_r, z4_s, z4_r, out_sem,
):
    row = lax.axis_index("rows")
    col = lax.axis_index("cols")
    y, z = row % NY, row // NY
    x, core = col // 2, col % 2

    def at_y(d):
        return (z * NY + (y + d) % NY, col)

    def at_z(d):
        return (((z + d) % NZ) * NY + y, col)

    def at_x(d):
        return (row, ((x + d) % NX) * 2 + core)

    other = (row, x * 2 + 1 - core)

    def remote(src, dst, send, recv, device):
        return pltpu.make_async_remote_copy(
            src_ref=src, dst_ref=dst, send_sem=send, recv_sem=recv, device_id=device, device_id_type=MESH
        )

    load = pltpu.make_async_copy(a_hbm, av, load_sem)
    load.start()

    barrier = pltpu.get_barrier_semaphore()

    def greet(device):
        pl.semaphore_signal(barrier, inc=1, device_id=device, device_id_type=MESH)

    each(NY - 1, lambda d: greet(at_y(d)))
    each(NZ - 1, lambda d: greet(at_z(d)))
    each(NX - 1, lambda d: greet(at_x(d)))
    greet(other)
    load.wait()
    pl.semaphore_wait(barrier, (NY - 1) + (NZ - 1) + (NX - 1) + 1)

    def chunk(i):
        return pt.at[pl.ds(2 * core, 2), pl.ds(pl.multiple_of(i * CH, CH), CH), :]

    def ring(i, d):
        return remote(chunk(i), chunk(i), ring_s.at[i], ring_r.at[i], at_x(d))

    def across(i):
        return remote(chunk(i), chunk(i), core_s.at[i], core_r.at[i], other)

    half = NCH // 2

    def loop(count, body):
        def step(i, carry):
            body(i)
            return carry

        lax.fori_loop(0, count, step, 0)

    @pl.when(x == 0)
    def _():
        for h in range(2):
            pt[2 * core + h] = av[pl.ds(h, ROWS, stride=TILES), :]

        def send(i):
            ring(i, 1).start()
            ring(half + i, NX - 1).start()
            across(i).start()
            across(half + i).start()

        loop(half, send)

    @pl.when(x == 1)
    def _():
        def first(i):
            ring(i, 1).wait_recv()
            ring(i, 1).start()
            across(i).start()

        def second(i):
            ring(half + i, 1).wait_recv()
            across(half + i).start()

        loop(half, first)
        loop(half, second)

    @pl.when(x == 2)
    def _():
        def both(i):
            ring(i, 1).wait_recv()
            ring(i, 1).start()
            across(i).start()
            ring(half + i, 1).wait_recv()
            ring(half + i, NX - 1).start()
            across(half + i).start()

        loop(half, both)

    @pl.when(x == 3)
    def _():
        def first(i):
            ring(half + i, 1).wait_recv()
            ring(half + i, NX - 1).start()
            across(half + i).start()

        def second(i):
            ring(i, 1).wait_recv()
            across(i).start()

        loop(half, first)
        loop(half, second)

    loop(NCH, lambda i: across(i).wait_recv())

    left = pt[x]
    for h in range(2):
        gs[h] = dot(left, pt[2 * core + h], ((0,), (0,)))

    def gram_y(d):
        return remote(gs, gy.at[y], gy_s.at[d - 1], gy_r.at[d - 1], at_y(d))

    exchange(NY - 1, gram_y)
    gy[y] = gs[...]

    panels = [split(jnp.concatenate([pt[q] for q in range(4)], axis=1))]

    def local_products(first, last):
        for t in range(first, last):
            gl[t] = dot3(panels[0], split(av[pl.ds(t, ROWS, stride=TILES), :]), ((0,), (0,)))

    local_products(0, 2)
    arrived(NY - 1, gram_y)
    gsum[...] = (gy[0] + gy[1]) + (gy[2] + gy[3])

    def rows16(ref, index):
        return ref.at[:, pl.ds(pl.multiple_of(index * 16, 16), 16), :]

    def gram_z(d):
        return remote(rows16(gsum, (z + d) % NZ), gz.at[z], gz_s.at[d - 1], gz_r.at[d - 1], at_z(d))

    exchange(NZ - 1, gram_z)
    gz[z] = gsum[:, pl.ds(pl.multiple_of(z * 16, 16), 16), :]
    local_products(2, 4)
    arrived(NZ - 1, gram_z)

    def gram_piece():
        return gram.at[x, pl.ds(2 * core, 2), pl.ds(pl.multiple_of(z * 16, 16), 16), :]

    total = gz[0]
    for i in range(1, NZ):
        total = total + gz[i]
    gram[x, pl.ds(2 * core, 2), pl.ds(pl.multiple_of(z * 16, 16), 16), :] = total

    def gram_all(d):
        return remote(gram_piece(), gram_piece(), ga_s.at[d - 1], ga_r.at[d - 1], at_z(d))

    exchange(NZ - 1, gram_all)
    local_products(4, 6)
    arrived(NZ - 1, gram_all)

    def gram_block(index):
        return gram.at[index, pl.ds(2 * core, 2), :, :]

    def gram_x(d):
        return remote(gram_block(x), gram_block(x), gx_s.at[d - 1], gx_r.at[d - 1], at_x(d))

    def gram_core(d):
        index = (x + NX - d) % NX
        return remote(gram_block(index), gram_block(index), gc_s.at[d], gc_r.at[d], other)

    exchange(NX - 1, gram_x)
    gram_core(0).start()
    local_products(6, 8)

    def rows_of(ref, lo, hi, index, size):
        return ref.at[lo:hi, pl.ds(pl.multiple_of(index * size, size), size), :]

    def y1(d):
        return remote(rows_of(gl, 0, TY, (y + d) % NY, 128), ry.at[d - 1], y1_s.at[d - 1], y1_r.at[d - 1], at_y(d))

    def z1(d):
        return remote(rows_of(gl, TY, TILES, (z + d) % NZ, 64), rz1.at[d - 1], z1_s.at[d - 1], z1_r.at[d - 1], at_z(d))

    exchange(NY - 1, y1)
    exchange(NZ - 1, z1)

    def pass_on(d):
        gram_x(d).wait_recv()
        gram_core(d).start()

    each(NX - 1, pass_on)

    arrived(NY - 1, y1)
    sy[...] = (gl[0:TY, pl.ds(pl.multiple_of(y * 128, 128), 128), :] + ry[0]) + (ry[1] + ry[2])

    def z2(d):
        return remote(rows_of(sy, 0, TY, (z + d) % NZ, 16), rz2.at[d - 1], z2_s.at[d - 1], z2_r.at[d - 1], at_z(d))

    exchange(NZ - 1, z2)
    arrived(NZ - 1, z1)
    total = gl[TY:TILES, pl.ds(pl.multiple_of(z * 64, 64), 64), :]
    for i in range(NZ - 1):
        total = total + rz1[i]
    sz[...] = total

    def y2(d):
        return remote(rows_of(sz, 0, TILES - TY, (y + d) % NY, 16), ry2.at[d - 1], y2_s.at[d - 1], y2_r.at[d - 1], at_y(d))

    exchange(NY - 1, y2)
    arrived(NZ - 1, z2)
    total = sy[:, pl.ds(pl.multiple_of(z * 16, 16), 16), :]
    for i in range(NZ - 1):
        total = total + rz2[i]
    gf[0:TY, pl.ds(pl.multiple_of((y * NZ + z) * 16, 16), 16), :] = total

    def z3(d):
        piece = rows_of(gf, 0, TY, y * NZ + z, 16)
        return remote(piece, piece, z3_s.at[d - 1], z3_r.at[d - 1], at_z(d))

    exchange(NZ - 1, z3)
    arrived(NY - 1, y2)
    total = sz[:, pl.ds(pl.multiple_of(y * 16, 16), 16), :]
    for i in range(NY - 1):
        total = total + ry2[i]
    gf[TY:TILES, pl.ds(pl.multiple_of((z * NY + y) * 16, 16), 16), :] = total

    def y3(d):
        piece = rows_of(gf, TY, TILES, z * NY + y, 16)
        return remote(piece, piece, y3_s.at[d - 1], y3_r.at[d - 1], at_y(d))

    exchange(NY - 1, y3)
    arrived(NZ - 1, z3)

    def y4(d):
        piece = rows_of(gf, 0, TY, y, 128)
        return remote(piece, piece, y4_s.at[d - 1], y4_r.at[d - 1], at_y(d))

    exchange(NY - 1, y4)
    arrived(NY - 1, y3)

    def z4(d):
        piece = rows_of(gf, TY, TILES, z, 64)
        return remote(piece, piece, z4_s.at[d - 1], z4_r.at[d - 1], at_z(d))

    exchange(NZ - 1, z4)
    for d in range(NX):
        gram_core(d).wait_recv()
    arrived(NY - 1, y4)
    arrived(NZ - 1, z4)

    outs = [
        pltpu.make_async_copy(src, dst, out_sem.at[i])
        for i, (src, dst) in enumerate([(pt, p_hbm), (gram, gram_hbm), (gf, g_hbm)])
    ]
    for copy in outs:
        copy.start()

    @pl.when(x == 0)
    def _():
        loop(half, lambda i: ring(i, 1).wait_send())
        loop(half, lambda i: ring(half + i, 1).wait_send())

    @pl.when(x == 1)
    def _():
        loop(half, lambda i: ring(i, 1).wait_send())

    @pl.when(x == 2)
    def _():
        loop(half, lambda i: ring(i, 1).wait_send())
        loop(half, lambda i: ring(half + i, 1).wait_send())

    @pl.when(x == 3)
    def _():
        loop(half, lambda i: ring(half + i, 1).wait_send())

    loop(NCH, lambda i: across(i).wait_send())
    for count, make in (
        (NY - 1, gram_y), (NZ - 1, gram_z), (NZ - 1, gram_all), (NX - 1, gram_x),
        (NY - 1, y1), (NZ - 1, z1), (NZ - 1, z2), (NY - 1, y2), (NZ - 1, z3), (NY - 1, y3), (NY - 1, y4), (NZ - 1, z4),
    ):
        sent(count, make)
    for d in range(NX):
        gram_core(d).wait_send()
    for copy in outs:
        copy.wait()


def gather_products(flat):
    dma = pltpu.SemaphoreType.DMA
    tz = TILES - TY
    y_pair = [dma((NY - 1,)), dma((NY - 1,))]
    z_pair = [dma((NZ - 1,)), dma((NZ - 1,))]
    x_pair = [dma((NX - 1,)), dma((NX - 1,))]
    any_space = pl.BlockSpec(memory_space=pl.ANY)
    return pl.pallas_call(
        gather_kernel,
        out_shape=(
            jax.ShapeDtypeStruct((4, ROWS, B), F32),
            jax.ShapeDtypeStruct((4, 4, B, B), F32),
            jax.ShapeDtypeStruct((TILES, WIDTH, B), F32),
        ),
        in_specs=[any_space],
        out_specs=(any_space,) * 3,
        scratch_shapes=[
            pltpu.VMEM((ROWS * TILES, B), F32),
            pltpu.VMEM((4, ROWS, B), F32),
            pltpu.VMEM((2, B, B), F32),
            pltpu.VMEM((NY, 2, B, B), F32),
            pltpu.VMEM((2, B, B), F32),
            pltpu.VMEM((NZ, 2, 16, B), F32),
            pltpu.VMEM((4, 4, B, B), F32),
            pltpu.VMEM((TILES, WIDTH, B), F32),
            pltpu.VMEM((TILES, WIDTH, B), F32),
            pltpu.VMEM((NY - 1, TY, 128, B), F32),
            pltpu.VMEM((TY, 128, B), F32),
            pltpu.VMEM((NZ - 1, TY, 16, B), F32),
            pltpu.VMEM((NZ - 1, tz, 64, B), F32),
            pltpu.VMEM((tz, 64, B), F32),
            pltpu.VMEM((NY - 1, tz, 16, B), F32),
            dma,
            dma((NCH,)), dma((NCH,)), dma((NCH,)), dma((NCH,)),
            *y_pair, *z_pair, *z_pair, *x_pair, dma((NX,)), dma((NX,)),
            *y_pair, *z_pair, *z_pair, *y_pair, *z_pair, *y_pair, *y_pair, *z_pair,
            dma((3,)),
        ],
        compiler_params=pltpu.CompilerParams(
            collective_id=0, has_side_effects=True, vmem_limit_bytes=48 << 20
        ),
        name="gather_products",
    )(flat)


def factor_kernel(gram_ref, m_ref, d_ref):
    for k in range(WIDTH // B):
        for t in range(WIDTH // B):
            block = gram_ref[k, t] if t >= k else jnp.zeros((B, B), F32)
            m_ref[B * k : B * (k + 1), B * t : B * (t + 1)] = block
    chol_inv(m_ref, d_ref)


def factor(gram):
    return pl.pallas_call(
        factor_kernel,
        out_shape=jax.ShapeDtypeStruct((WIDTH, WIDTH), F32),
        scratch_shapes=[pltpu.VMEM((B, B), F32)],
        compiler_params=pltpu.CompilerParams(vmem_limit_bytes=32 << 20),
        name="factor",
    )(gram)


def project_kernel(a_ref, p_ref, m_ref, g_ref, rows_ref, basis_ref, trail_ref, wh, wl):
    rows = p_ref.shape[1]
    inverse = split(m_ref[...])

    @pl.when(pl.program_id(0) == 0)
    def _():
        for t in range(TILES):
            w = dot3(inverse, split(g_ref[t]), ((1,), (0,)))
            rows_ref[pl.ds(t, WIDTH, stride=TILES), :] = w
            wh[t], wl[t] = split(w)

    panel = split(jnp.concatenate([p_ref[q] for q in range(4)], axis=1))
    basis = dot3(panel, inverse, ((1,), (1,)))
    for q in range(4):
        basis_ref[pl.ds((q % 2) * 2 + q // 2, rows, stride=4), :] = basis[:, B * q : B * (q + 1)]
    pair = split(basis)
    for t in range(TILES):
        spot = pl.ds(t, rows, stride=TILES)
        trail_ref[spot, :] = a_ref[spot, :] - dot3(pair, (wh[t], wl[t]), ((1,), (0,)))


def project(flat, panels, inverse, products):
    steps = 4
    rows = ROWS // steps
    return pl.pallas_call(
        project_kernel,
        grid=(steps,),
        out_shape=(
            jax.ShapeDtypeStruct((WIDTH * TILES, B), F32),
            jax.ShapeDtypeStruct((ROWS * 4, B), F32),
            jax.ShapeDtypeStruct((ROWS * TILES, B), F32),
        ),
        in_specs=[
            pl.BlockSpec((rows * TILES, B), lambda i: (i, 0)),
            pl.BlockSpec((4, rows, B), lambda i: (0, i, 0)),
            pl.BlockSpec((WIDTH, WIDTH), lambda i: (0, 0)),
            pl.BlockSpec((TILES, WIDTH, B), lambda i: (0, 0, 0)),
        ],
        out_specs=(
            pl.BlockSpec((WIDTH * TILES, B), lambda i: (0, 0)),
            pl.BlockSpec((rows * 4, B), lambda i: (i, 0)),
            pl.BlockSpec((rows * TILES, B), lambda i: (i, 0)),
        ),
        scratch_shapes=[pltpu.VMEM((TILES, WIDTH, B), BF16)] * 2,
        compiler_params=pltpu.CompilerParams(vmem_limit_bytes=40 << 20),
        name="project",
    )(flat, panels, inverse, products)


def on_device(features):
    flat = features.reshape(ROWS * TILES, B)
    panels, gram, products = gather_products(flat)
    inverse = factor(gram)
    factor_rows, basis, trailing = project(flat, panels, inverse, products)
    basis = basis.reshape(ROWS, 2, 2, B).transpose(0, 2, 1, 3).reshape(ROWS, 2, 256)
    return (factor_rows.reshape(WIDTH, 4, 1, 256), basis, trailing.reshape(features.shape))


def solution(mesh):
    placed = (P("rows", None, "cols", None),)
    return jax.shard_map(
        on_device,
        mesh=mesh,
        in_specs=placed,
        out_specs=(
            P(None, None, "cols", None),
            P("rows", None, None),
            P("rows", None, "cols", None),
        ),
        check_vma=False,
    )
```

```python
import jax
import jax.numpy as jnp
from jax import lax
from jax.experimental import pallas as pl
from jax.experimental.pallas import tpu as pltpu
from jax.sharding import PartitionSpec as P

HIGHEST = lax.Precision.HIGHEST
F32 = jnp.float32
BF16 = jnp.bfloat16
MESH = pl.DeviceIdType.MESH

NY = 4
NZ = 8
NX = 4
ROWS = 1024
WIDTH = 512
B = 128
GR = 8
TILES = 8
TY = 6
CH = 64
NCH = ROWS // CH


def dot(a, b, dims):
    return lax.dot_general(a, b, (dims, ((), ())), precision=HIGHEST, preferred_element_type=F32)


def split(value):
    high = value.astype(BF16)
    return high, (value - high.astype(F32)).astype(BF16)


def dot3(a, b, dims):
    def one(u, v):
        return lax.dot_general(u, v, (dims, ((), ())), preferred_element_type=F32)

    return one(a[0], b[0]) + (one(a[0], b[1]) + one(a[1], b[0]))

def rows_bcast(x, j):
    return jnp.broadcast_to(x[j:j + 1, :], x.shape)

def lane_bcast(x, c):
    return jnp.broadcast_to(x[:, c:c + 1], x.shape)

def leaf(x_ref):
    n = B // GR
    lane = lax.broadcasted_iota(jnp.int32, (GR, B), 1)
    sub = lax.broadcasted_iota(jnp.int32, (GR, B), 0)
    x = [x_ref[GR * t:GR * (t + 1), :] for t in range(n)]
    for g in range(n):
        base = GR * g
        cur = x[g]
        v = [lane_bcast(cur, base + c) for c in range(GR)]
        in_group = (lane >= base) & (lane < base + GR)
        scale, mult, rows = [], {}, []
        for j in range(GR):
            r = lax.rsqrt(rows_bcast(v[j], j))
            w = jnp.where(sub > j, v[j] * r, 0.0)
            row = jnp.where(lane == base + j, r, rows_bcast(cur, j) * r)
            cur = jnp.where(sub == j, row, jnp.where((lane == base + j) & (sub > j), 0.0, cur) - w * row)
            for c in range(j + 1, GR):
                m = rows_bcast(v[c], j) * r
                mult[j, c] = m
                v[c] = v[c] - w * m
            scale.append(r)
            rows.append(jnp.where(in_group & (lane > base + j), 0.0, row))
        x[g] = cur
        for t in range(g + 1, n):
            xt = x[t]
            u = [lane_bcast(xt, base + c) for c in range(GR)]
            xt = jnp.where(in_group, 0.0, xt)
            for j in range(GR):
                w = u[j] * scale[j]
                for c in range(j + 1, GR):
                    u[c] = u[c] - w * mult[j, c]
                xt = xt - w * rows[j]
            x[t] = xt
    for t in range(n):
        x_ref[GR * t:GR * (t + 1), :] = x[t]

def factor_step(k, m_ref, d_ref):
    size = m_ref.shape[0]
    sl = slice(B * k, B * (k + 1))
    d_ref[...] = m_ref[sl, sl]
    leaf(d_ref)
    ri = lax.broadcasted_iota(jnp.int32, (B, B), 0)
    ci = lax.broadcasted_iota(jnp.int32, (B, B), 1)
    m = jnp.where(ri >= ci, d_ref[...], 0.0)
    m_ref[sl, sl] = m
    if k:
        left = dot(m, m_ref[sl, : B * k], ((1,), (0,)))
        m_ref[sl, : B * k] = left
    if B * (k + 1) < size:
        rest = slice(B * (k + 1), size)
        up = dot(m, m_ref[sl, rest], ((1,), (0,)))
        m_ref[sl, rest] = jnp.zeros_like(up)
        m_ref[rest, rest] = m_ref[rest, rest] - dot(up, up, ((0,), (0,)))
        m_ref[rest, sl] = -dot(up, m, ((0,), (0,)))
        if k:
            m_ref[rest, : B * k] = m_ref[rest, : B * k] - dot(up, left, ((0,), (0,)))


def each(count, body):
    def step(i, carry):
        body(i + 1)
        return carry

    lax.fori_loop(0, count, step, 0)


def exchange(count, make):
    each(count, lambda d: make(d).start())


def arrived(count, make):
    each(count, lambda d: make(d).wait_recv())


def sent(count, make):
    each(count, lambda d: make(d).wait_send())


def gather_kernel(
    a_hbm, p_hbm, m_hbm, g_hbm,
    av, pt, ph, pl_, mm, dd, gs, gy, gsum, gz, gram, gl, gf, ry, sy, rz2, rz1, sz, ry2,
    load_sem, ring_s, ring_r, core_s, core_r, gy_s, gy_r, gz_s, gz_r, ga_s, ga_r, gx_s, gx_r, gc_s, gc_r,
    y1_s, y1_r, z1_s, z1_r, z2_s, z2_r, y2_s, y2_r, z3_s, z3_r, y3_s, y3_r, y4_s, y4_r, z4_s, z4_r, out_sem,
):
    row = lax.axis_index("rows")
    col = lax.axis_index("cols")
    y, z = row % NY, row // NY
    x, core = col // 2, col % 2

    def at_y(d):
        return (z * NY + (y + d) % NY, col)

    def at_z(d):
        return (((z + d) % NZ) * NY + y, col)

    def at_x(d):
        return (row, ((x + d) % NX) * 2 + core)

    other = (row, x * 2 + 1 - core)

    def remote(src, dst, send, recv, device):
        return pltpu.make_async_remote_copy(
            src_ref=src, dst_ref=dst, send_sem=send, recv_sem=recv, device_id=device, device_id_type=MESH
        )

    def load(i):
        part = pl.ds(i * CH * TILES, CH * TILES)
        return pltpu.make_async_copy(a_hbm.at[part, :], av.at[part, :], load_sem.at[i])

    half = NCH // 2
    for i in range(half):
        load(i).start()
        load(half + i).start()

    barrier = pltpu.get_barrier_semaphore()

    def greet(device):
        pl.semaphore_signal(barrier, inc=1, device_id=device, device_id_type=MESH)

    each(NY - 1, lambda d: greet(at_y(d)))
    each(NZ - 1, lambda d: greet(at_z(d)))
    each(NX - 1, lambda d: greet(at_x(d)))
    greet(other)
    pl.semaphore_wait(barrier, (NY - 1) + (NZ - 1) + (NX - 1) + 1)

    def chunk(i):
        return pt.at[pl.ds(2 * core, 2), pl.ds(pl.multiple_of(i * CH, CH), CH), :]

    def ring(i, d):
        return remote(chunk(i), chunk(i), ring_s.at[i], ring_r.at[i], at_x(d))

    def across(i):
        return remote(chunk(i), chunk(i), core_s.at[i], core_r.at[i], other)

    def loop(count, body):
        def step(i, carry):
            body(i)
            return carry

        lax.fori_loop(0, count, step, 0)

    @pl.when(x == 0)
    def _():
        for i in range(half):
            for j in (i, half + i):
                load(j).wait()
                for h in range(2):
                    pt[2 * core + h, CH * j : CH * (j + 1), :] = av[pl.ds(CH * TILES * j + h, CH, stride=TILES), :]
            ring(i, 1).start()
            ring(half + i, NX - 1).start()
            across(i).start()
            across(half + i).start()

    @pl.when(x > 0)
    def _():
        for i in range(NCH):
            load(i).wait()

    @pl.when(x == 1)
    def _():
        def first(i):
            ring(i, 1).wait_recv()
            ring(i, 1).start()
            across(i).start()

        def second(i):
            ring(half + i, 1).wait_recv()
            across(half + i).start()

        loop(half, first)
        loop(half, second)

    @pl.when(x == 2)
    def _():
        def both(i):
            ring(i, 1).wait_recv()
            ring(i, 1).start()
            across(i).start()
            ring(half + i, 1).wait_recv()
            ring(half + i, NX - 1).start()
            across(half + i).start()

        loop(half, both)

    @pl.when(x == 3)
    def _():
        def first(i):
            ring(half + i, 1).wait_recv()
            ring(half + i, NX - 1).start()
            across(half + i).start()

        def second(i):
            ring(i, 1).wait_recv()
            across(i).start()

        loop(half, first)
        loop(half, second)

    loop(NCH, lambda i: across(i).wait_recv())

    left = pt[x]
    for h in range(2):
        gs[h] = dot(left, pt[2 * core + h], ((0,), (0,)))

    def gram_y(d):
        return remote(gs, gy.at[y], gy_s.at[d - 1], gy_r.at[d - 1], at_y(d))

    exchange(NY - 1, gram_y)
    gy[y] = gs[...]

    for q in range(4):
        high, low = split(pt[q])
        ph[B * q : B * (q + 1), :] = high.T
        pl_[B * q : B * (q + 1), :] = low.T

    def local_products(t):
        tiles = [av[pl.ds(t + h, ROWS, stride=TILES), :] for h in range(2)]
        out = dot3((ph[...], pl_[...]), split(jnp.concatenate(tiles, axis=1)), ((1,), (0,)))
        gl[t] = out[:, :B]
        gl[t + 1] = out[:, B:]

    def rows_of(ref, lo, hi, index, size):
        return ref.at[lo:hi, pl.ds(pl.multiple_of(index * size, size), size), :]

    def y1(pair):
        lo = 2 * pair

        def make(d):
            src = rows_of(gl, lo, lo + 2, (y + d) % NY, 128)
            return remote(src, ry.at[d - 1, lo : lo + 2], y1_s.at[pair, d - 1], y1_r.at[pair, d - 1], at_y(d))

        return make

    def z1(d):
        return remote(rows_of(gl, TY, TILES, (z + d) % NZ, 64), rz1.at[d - 1], z1_s.at[d - 1], z1_r.at[d - 1], at_z(d))

    local_products(0)
    exchange(NY - 1, y1(0))
    local_products(6)
    exchange(NZ - 1, z1)
    arrived(NY - 1, gram_y)
    gsum[...] = (gy[0] + gy[1]) + (gy[2] + gy[3])

    def rows16(ref, index):
        return ref.at[:, pl.ds(pl.multiple_of(index * 16, 16), 16), :]

    def gram_z(d):
        return remote(rows16(gsum, (z + d) % NZ), gz.at[z], gz_s.at[d - 1], gz_r.at[d - 1], at_z(d))

    exchange(NZ - 1, gram_z)
    gz[z] = gsum[:, pl.ds(pl.multiple_of(z * 16, 16), 16), :]
    local_products(2)
    exchange(NY - 1, y1(1))
    arrived(NZ - 1, gram_z)

    def gram_piece():
        return gram.at[x, pl.ds(2 * core, 2), pl.ds(pl.multiple_of(z * 16, 16), 16), :]

    total = gz[0]
    for i in range(1, NZ):
        total = total + gz[i]
    gram[x, pl.ds(2 * core, 2), pl.ds(pl.multiple_of(z * 16, 16), 16), :] = total

    def gram_all(d):
        return remote(gram_piece(), gram_piece(), ga_s.at[d - 1], ga_r.at[d - 1], at_z(d))

    exchange(NZ - 1, gram_all)
    local_products(4)
    exchange(NY - 1, y1(2))
    arrived(NZ - 1, gram_all)

    def gram_block(index):
        return gram.at[index, pl.ds(2 * core, 2), :, :]

    def gram_x(d):
        return remote(gram_block(x), gram_block(x), gx_s.at[d - 1], gx_r.at[d - 1], at_x(d))

    def gram_core(d):
        index = (x + NX - d) % NX
        return remote(gram_block(index), gram_block(index), gc_s.at[d], gc_r.at[d], other)

    exchange(NX - 1, gram_x)
    gram_core(0).start()

    def pass_on(d):
        gram_x(d).wait_recv()
        gram_core(d).start()

    each(NX - 1, pass_on)

    for pair in range(TY // 2):
        arrived(NY - 1, y1(pair))
    sy[...] = (gl[0:TY, pl.ds(pl.multiple_of(y * 128, 128), 128), :] + ry[0]) + (ry[1] + ry[2])

    def z2(d):
        return remote(rows_of(sy, 0, TY, (z + d) % NZ, 16), rz2.at[d - 1], z2_s.at[d - 1], z2_r.at[d - 1], at_z(d))

    exchange(NZ - 1, z2)
    arrived(NZ - 1, z1)
    total = gl[TY:TILES, pl.ds(pl.multiple_of(z * 64, 64), 64), :]
    for i in range(NZ - 1):
        total = total + rz1[i]
    sz[...] = total

    def y2(d):
        return remote(rows_of(sz, 0, TILES - TY, (y + d) % NY, 16), ry2.at[d - 1], y2_s.at[d - 1], y2_r.at[d - 1], at_y(d))

    exchange(NY - 1, y2)

    for d in range(NX):
        gram_core(d).wait_recv()
    for k in range(4):
        for t in range(4):
            mm[B * k : B * (k + 1), B * t : B * (t + 1)] = gram[k, t] if t >= k else jnp.zeros((B, B), F32)
    factor_step(0, mm, dd)

    arrived(NZ - 1, z2)
    total = sy[:, pl.ds(pl.multiple_of(z * 16, 16), 16), :]
    for i in range(NZ - 1):
        total = total + rz2[i]
    gf[0:TY, pl.ds(pl.multiple_of((y * NZ + z) * 16, 16), 16), :] = total

    def z3(d):
        piece = rows_of(gf, 0, TY, y * NZ + z, 16)
        return remote(piece, piece, z3_s.at[d - 1], z3_r.at[d - 1], at_z(d))

    exchange(NZ - 1, z3)
    arrived(NY - 1, y2)
    total = sz[:, pl.ds(pl.multiple_of(y * 16, 16), 16), :]
    for i in range(NY - 1):
        total = total + ry2[i]
    gf[TY:TILES, pl.ds(pl.multiple_of((z * NY + y) * 16, 16), 16), :] = total

    def y3(d):
        piece = rows_of(gf, TY, TILES, z * NY + y, 16)
        return remote(piece, piece, y3_s.at[d - 1], y3_r.at[d - 1], at_y(d))

    exchange(NY - 1, y3)
    factor_step(1, mm, dd)
    arrived(NZ - 1, z3)

    def y4(d):
        piece = rows_of(gf, 0, TY, y, 128)
        return remote(piece, piece, y4_s.at[d - 1], y4_r.at[d - 1], at_y(d))

    exchange(NY - 1, y4)
    arrived(NY - 1, y3)

    def z4(d):
        piece = rows_of(gf, TY, TILES, z, 64)
        return remote(piece, piece, z4_s.at[d - 1], z4_r.at[d - 1], at_z(d))

    exchange(NZ - 1, z4)
    factor_step(2, mm, dd)
    factor_step(3, mm, dd)
    arrived(NY - 1, y4)
    arrived(NZ - 1, z4)

    outs = [
        pltpu.make_async_copy(src, dst, out_sem.at[i])
        for i, (src, dst) in enumerate([(pt, p_hbm), (mm, m_hbm), (gf, g_hbm)])
    ]
    for copy in outs:
        copy.start()

    @pl.when(x == 0)
    def _():
        loop(half, lambda i: ring(i, 1).wait_send())
        loop(half, lambda i: ring(half + i, 1).wait_send())

    @pl.when(x == 1)
    def _():
        loop(half, lambda i: ring(i, 1).wait_send())

    @pl.when(x == 2)
    def _():
        loop(half, lambda i: ring(i, 1).wait_send())
        loop(half, lambda i: ring(half + i, 1).wait_send())

    @pl.when(x == 3)
    def _():
        loop(half, lambda i: ring(half + i, 1).wait_send())

    loop(NCH, lambda i: across(i).wait_send())
    for count, make in (
        (NY - 1, gram_y), (NZ - 1, gram_z), (NZ - 1, gram_all), (NX - 1, gram_x),
        (NY - 1, y1(0)), (NY - 1, y1(1)), (NY - 1, y1(2)), (NZ - 1, z1), (NZ - 1, z2), (NY - 1, y2), (NZ - 1, z3), (NY - 1, y3), (NY - 1, y4), (NZ - 1, z4),
    ):
        sent(count, make)
    for d in range(NX):
        gram_core(d).wait_send()
    for copy in outs:
        copy.wait()


def gather_products(flat):
    dma = pltpu.SemaphoreType.DMA
    tz = TILES - TY
    y_pair = [dma((NY - 1,)), dma((NY - 1,))]
    z_pair = [dma((NZ - 1,)), dma((NZ - 1,))]
    x_pair = [dma((NX - 1,)), dma((NX - 1,))]
    any_space = pl.BlockSpec(memory_space=pl.ANY)
    return pl.pallas_call(
        gather_kernel,
        out_shape=(
            jax.ShapeDtypeStruct((4, ROWS, B), F32),
            jax.ShapeDtypeStruct((WIDTH, WIDTH), F32),
            jax.ShapeDtypeStruct((TILES, WIDTH, B), F32),
        ),
        in_specs=[any_space],
        out_specs=(any_space,) * 3,
        scratch_shapes=[
            pltpu.VMEM((ROWS * TILES, B), F32),
            pltpu.VMEM((4, ROWS, B), F32),
            pltpu.VMEM((WIDTH, ROWS), BF16),
            pltpu.VMEM((WIDTH, ROWS), BF16),
            pltpu.VMEM((WIDTH, WIDTH), F32),
            pltpu.VMEM((B, B), F32),
            pltpu.VMEM((2, B, B), F32),
            pltpu.VMEM((NY, 2, B, B), F32),
            pltpu.VMEM((2, B, B), F32),
            pltpu.VMEM((NZ, 2, 16, B), F32),
            pltpu.VMEM((4, 4, B, B), F32),
            pltpu.VMEM((TILES, WIDTH, B), F32),
            pltpu.VMEM((TILES, WIDTH, B), F32),
            pltpu.VMEM((NY - 1, TY, 128, B), F32),
            pltpu.VMEM((TY, 128, B), F32),
            pltpu.VMEM((NZ - 1, TY, 16, B), F32),
            pltpu.VMEM((NZ - 1, tz, 64, B), F32),
            pltpu.VMEM((tz, 64, B), F32),
            pltpu.VMEM((NY - 1, tz, 16, B), F32),
            dma((NCH,)),
            dma((NCH,)), dma((NCH,)), dma((NCH,)), dma((NCH,)),
            *y_pair, *z_pair, *z_pair, *x_pair, dma((NX,)), dma((NX,)),
            dma((TY // 2, NY - 1)), dma((TY // 2, NY - 1)), *z_pair, *z_pair, *y_pair, *z_pair, *y_pair, *y_pair, *z_pair,
            dma((3,)),
        ],
        compiler_params=pltpu.CompilerParams(
            collective_id=0, has_side_effects=True, vmem_limit_bytes=48 << 20
        ),
        name="gather_products",
    )(flat)


def project_kernel(a_ref, p_ref, m_ref, g_ref, rows_ref, basis_ref, trail_ref, wh, wl):
    rows = p_ref.shape[1]
    inverse = split(m_ref[...])
    half = WIDTH // 2

    @pl.when(pl.program_id(0) == 0)
    def _():
        for t in range(0, TILES, 2):
            g = split(jnp.concatenate([g_ref[t], g_ref[t + 1]], axis=1))
            upper = dot3([v[:half, :half] for v in inverse], [v[:half] for v in g], ((1,), (0,)))
            lower = dot3([v[half:] for v in inverse], g, ((1,), (0,)))
            w = jnp.concatenate([upper, lower], axis=0)
            for h in range(2):
                rows_ref[pl.ds(t + h, WIDTH, stride=TILES), :] = w[:, B * h : B * (h + 1)]
            wh[t // 2], wl[t // 2] = split(w)

    panel = split(jnp.concatenate([p_ref[q] for q in range(4)], axis=1))
    basis = dot3(panel, inverse, ((1,), (1,)))
    for q in range(4):
        basis_ref[pl.ds((q % 2) * 2 + q // 2, rows, stride=4), :] = basis[:, B * q : B * (q + 1)]
    pair = split(basis)
    for t in range(0, TILES, 2):
        part = dot3(pair, (wh[t // 2], wl[t // 2]), ((1,), (0,)))
        for h in range(2):
            spot = pl.ds(t + h, rows, stride=TILES)
            trail_ref[spot, :] = a_ref[spot, :] - part[:, B * h : B * (h + 1)]


def project(flat, panels, inverse, products):
    steps = 4
    rows = ROWS // steps
    return pl.pallas_call(
        project_kernel,
        grid=(steps,),
        out_shape=(
            jax.ShapeDtypeStruct((WIDTH * TILES, B), F32),
            jax.ShapeDtypeStruct((ROWS * 4, B), F32),
            jax.ShapeDtypeStruct((ROWS * TILES, B), F32),
        ),
        in_specs=[
            pl.BlockSpec((rows * TILES, B), lambda i: (i, 0)),
            pl.BlockSpec((4, rows, B), lambda i: (0, i, 0)),
            pl.BlockSpec((WIDTH, WIDTH), lambda i: (0, 0)),
            pl.BlockSpec((TILES, WIDTH, B), lambda i: (0, 0, 0)),
        ],
        out_specs=(
            pl.BlockSpec((WIDTH * TILES, B), lambda i: (0, 0)),
            pl.BlockSpec((rows * 4, B), lambda i: (i, 0)),
            pl.BlockSpec((rows * TILES, B), lambda i: (i, 0)),
        ),
        scratch_shapes=[pltpu.VMEM((TILES // 2, WIDTH, 2 * B), BF16)] * 2,
        compiler_params=pltpu.CompilerParams(vmem_limit_bytes=40 << 20),
        name="project",
    )(flat, panels, inverse, products)


def on_device(features):
    flat = features.reshape(ROWS * TILES, B)
    panels, inverse, products = gather_products(flat)
    factor_rows, basis, trailing = project(flat, panels, inverse, products)
    basis = basis.reshape(ROWS, 2, 2, B).transpose(0, 2, 1, 3).reshape(ROWS, 2, 256)
    return (factor_rows.reshape(WIDTH, 4, 1, 256), basis, trailing.reshape(features.shape))


def solution(mesh):
    placed = (P("rows", None, "cols", None),)
    return jax.shard_map(
        on_device,
        mesh=mesh,
        in_specs=placed,
        out_specs=(
            P(None, None, "cols", None),
            P("rows", None, None),
            P("rows", None, "cols", None),
        ),
        check_vma=False,
    )
```

```python
import jax
import jax.numpy as jnp
from jax import lax
from jax.experimental import pallas as pl
from jax.experimental.pallas import tpu as pltpu
from jax.sharding import PartitionSpec as P

HIGHEST = lax.Precision.HIGHEST
F32 = jnp.float32
BF16 = jnp.bfloat16
MESH = pl.DeviceIdType.MESH

NY = 4
NZ = 8
NX = 4
ROWS = 1024
WIDTH = 512
B = 128
GR = 8
TILES = 8
TY = 4
CH = 64
NCH = ROWS // CH


def dot(a, b, dims):
    return lax.dot_general(a, b, (dims, ((), ())), precision=HIGHEST, preferred_element_type=F32)


def split(value):
    high = value.astype(BF16)
    return high, (value - high.astype(F32)).astype(BF16)


def dot3(a, b, dims):
    def one(u, v):
        return lax.dot_general(u, v, (dims, ((), ())), preferred_element_type=F32)

    return one(a[0], b[0]) + (one(a[0], b[1]) + one(a[1], b[0]))

def rows_bcast(x, j):
    return jnp.broadcast_to(x[j:j + 1, :], x.shape)

def lane_bcast(x, c):
    return jnp.broadcast_to(x[:, c:c + 1], x.shape)

def leaf(x_ref, hook):
    n = B // GR
    lane = lax.broadcasted_iota(jnp.int32, (GR, B), 1)
    sub = lax.broadcasted_iota(jnp.int32, (GR, B), 0)
    x = [x_ref[GR * t:GR * (t + 1), :] for t in range(n)]
    for g in range(n):
        if hook is not None and g == n // 2:
            hook()
        base = GR * g
        cur = x[g]
        v = [lane_bcast(cur, base + c) for c in range(GR)]
        in_group = (lane >= base) & (lane < base + GR)
        scale, mult, rows = [], {}, []
        for j in range(GR):
            r = lax.rsqrt(rows_bcast(v[j], j))
            w = jnp.where(sub > j, v[j] * r, 0.0)
            row = jnp.where(lane == base + j, r, rows_bcast(cur, j) * r)
            cur = jnp.where(sub == j, row, jnp.where((lane == base + j) & (sub > j), 0.0, cur) - w * row)
            for c in range(j + 1, GR):
                m = rows_bcast(v[c], j) * r
                mult[j, c] = m
                v[c] = v[c] - w * m
            scale.append(r)
            rows.append(jnp.where(in_group & (lane > base + j), 0.0, row))
        x[g] = cur
        for t in range(g + 1, n):
            xt = x[t]
            u = [lane_bcast(xt, base + c) for c in range(GR)]
            xt = jnp.where(in_group, 0.0, xt)
            for j in range(GR):
                w = u[j] * scale[j]
                for c in range(j + 1, GR):
                    u[c] = u[c] - w * mult[j, c]
                xt = xt - w * rows[j]
            x[t] = xt
    for t in range(n):
        x_ref[GR * t:GR * (t + 1), :] = x[t]

def factor_step(k, m_ref, d_ref, hook=None):
    size = m_ref.shape[0]
    sl = slice(B * k, B * (k + 1))
    d_ref[...] = m_ref[sl, sl]
    leaf(d_ref, hook)
    ri = lax.broadcasted_iota(jnp.int32, (B, B), 0)
    ci = lax.broadcasted_iota(jnp.int32, (B, B), 1)
    m = jnp.where(ri >= ci, d_ref[...], 0.0)
    m_ref[sl, sl] = m
    if k:
        left = dot(m, m_ref[sl, : B * k], ((1,), (0,)))
        m_ref[sl, : B * k] = left
    if B * (k + 1) < size:
        rest = slice(B * (k + 1), size)
        up = dot(m, m_ref[sl, rest], ((1,), (0,)))
        m_ref[sl, rest] = jnp.zeros_like(up)
        m_ref[rest, rest] = m_ref[rest, rest] - dot(up, up, ((0,), (0,)))
        m_ref[rest, sl] = -dot(up, m, ((0,), (0,)))
        if k:
            m_ref[rest, : B * k] = m_ref[rest, : B * k] - dot(up, left, ((0,), (0,)))


def each(count, body):
    def step(i, carry):
        body(i + 1)
        return carry

    lax.fori_loop(0, count, step, 0)


def exchange(count, make):
    each(count, lambda d: make(d).start())


def arrived(count, make):
    each(count, lambda d: make(d).wait_recv())


def sent(count, make):
    each(count, lambda d: make(d).wait_send())


def gather_kernel(
    a_hbm, p_hbm, m_hbm, g_hbm,
    av, pt, ph, pl_, mm, dd, gs, gy, gsum, gz, gram, gl, gf, ry, sy, rz2, first_in, in_r, in_l, out_r, out_l, sz, ry2,
    load_sem, ring_s, ring_r, core_s, core_r, gy_s, gy_r, gz_s, gz_r, ga_s, ga_r, gx_s, gx_r, gc_s, gc_r,
    y1_s, y1_r, sum_s, sum_r, z2_s, z2_r, y2_s, y2_r, z3_s, z3_r, y3_s, y3_r, y4_s, y4_r, all_s, all_r, out_sem,
):
    row = lax.axis_index("rows")
    col = lax.axis_index("cols")
    y, z = row % NY, row // NY
    x, core = col // 2, col % 2

    def at_y(d):
        return (z * NY + (y + d) % NY, col)

    def at_z(d):
        return (((z + d) % NZ) * NY + y, col)

    def at_x(d):
        return (row, ((x + d) % NX) * 2 + core)

    other = (row, x * 2 + 1 - core)

    def remote(src, dst, send, recv, device):
        return pltpu.make_async_remote_copy(
            src_ref=src, dst_ref=dst, send_sem=send, recv_sem=recv, device_id=device, device_id_type=MESH
        )

    def load(i):
        part = pl.ds(i * CH * TILES, CH * TILES)
        return pltpu.make_async_copy(a_hbm.at[part, :], av.at[part, :], load_sem.at[i])

    half = NCH // 2
    for i in range(half):
        load(i).start()
        load(half + i).start()

    barrier = pltpu.get_barrier_semaphore()

    def greet(device):
        pl.semaphore_signal(barrier, inc=1, device_id=device, device_id_type=MESH)

    each(NY - 1, lambda d: greet(at_y(d)))
    each(NZ - 1, lambda d: greet(at_z(d)))
    each(NX - 1, lambda d: greet(at_x(d)))
    greet(other)
    pl.semaphore_wait(barrier, (NY - 1) + (NZ - 1) + (NX - 1) + 1)

    def chunk(i):
        return pt.at[pl.ds(2 * core, 2), pl.ds(pl.multiple_of(i * CH, CH), CH), :]

    def ring(i, d):
        return remote(chunk(i), chunk(i), ring_s.at[i], ring_r.at[i], at_x(d))

    def across(i):
        return remote(chunk(i), chunk(i), core_s.at[i], core_r.at[i], other)

    def loop(count, body):
        def step(i, carry):
            body(i)
            return carry

        lax.fori_loop(0, count, step, 0)

    @pl.when(x == 0)
    def _():
        for i in range(half):
            for j in (i, half + i):
                load(j).wait()
                for h in range(2):
                    pt[2 * core + h, CH * j : CH * (j + 1), :] = av[pl.ds(CH * TILES * j + h, CH, stride=TILES), :]
            ring(i, 1).start()
            ring(half + i, NX - 1).start()
            across(i).start()
            across(half + i).start()

    @pl.when(x > 0)
    def _():
        for i in range(NCH):
            load(i).wait()

    @pl.when(x == 1)
    def _():
        def first(i):
            ring(i, 1).wait_recv()
            ring(i, 1).start()
            across(i).start()

        def second(i):
            ring(half + i, 1).wait_recv()
            across(half + i).start()

        loop(half, first)
        loop(half, second)

    @pl.when(x == 2)
    def _():
        def both(i):
            ring(i, 1).wait_recv()
            ring(i, 1).start()
            across(i).start()
            ring(half + i, 1).wait_recv()
            ring(half + i, NX - 1).start()
            across(half + i).start()

        loop(half, both)

    @pl.when(x == 3)
    def _():
        def first(i):
            ring(half + i, 1).wait_recv()
            ring(half + i, NX - 1).start()
            across(half + i).start()

        def second(i):
            ring(i, 1).wait_recv()
            across(i).start()

        loop(half, first)
        loop(half, second)

    loop(NCH, lambda i: across(i).wait_recv())

    left = pt[x]
    for h in range(2):
        gs[h] = dot(left, pt[2 * core + h], ((0,), (0,)))

    def gram_y(d):
        return remote(gs, gy.at[y], gy_s.at[d - 1], gy_r.at[d - 1], at_y(d))

    exchange(NY - 1, gram_y)
    gy[y] = gs[...]

    for q in range(4):
        high, low = split(pt[q])
        ph[B * q : B * (q + 1), :] = high.T
        pl_[B * q : B * (q + 1), :] = low.T

    def local_products(t):
        tiles = [av[pl.ds(t + h, ROWS, stride=TILES), :] for h in range(2)]
        out = dot3((ph[...], pl_[...]), split(jnp.concatenate(tiles, axis=1)), ((1,), (0,)))
        gl[t] = out[:, :B]
        gl[t + 1] = out[:, B:]

    def rows_of(ref, lo, hi, index, size):
        return ref.at[lo:hi, pl.ds(pl.multiple_of(index * size, size), size), :]

    def y1(pair):
        lo = 2 * pair

        def make(d):
            src = rows_of(gl, lo, lo + 2, (y + d) % NY, 128)
            return remote(src, ry.at[d - 1, lo : lo + 2], y1_s.at[pair, d - 1], y1_r.at[pair, d - 1], at_y(d))

        return make

    ways = ((1, in_r, out_r), (NZ - 1, in_l, out_l))
    near = TY + (TILES - TY) // 2

    def block(lo, hi, index):
        return gl[lo:hi, pl.ds(pl.multiple_of((index % NZ) * 64, 64), 64), :]

    def z_sum(hop, way):
        to, into, out = ways[way]
        if hop == 0:
            lo, hi = (TY, near) if way == 0 else (near, TILES)
            src, dst = rows_of(gl, lo, hi, (z + 4) % NZ, 64), first_in.at[way]
        else:
            src, dst = out.at[hop - 1], into.at[hop - 1]
        return remote(src, dst, sum_s.at[way, hop], sum_r.at[way, hop], at_z(to))

    def z_hop(hop):
        for way, (to, into, out) in enumerate(ways):
            if hop > 0:
                z_sum(hop - 1, way).wait_recv()
                index = z + (4 - hop) if way == 0 else z + NZ - (4 - hop)
                low, high = block(TY, near, index), block(near, TILES, index)
                if hop == 1:
                    low, high = (low + first_in[0], high) if way == 0 else (low, high + first_in[1])
                else:
                    cut = near - TY
                    low, high = low + into[hop - 2, :cut], high + into[hop - 2, cut:]
                out[hop - 1, : near - TY] = low
                out[hop - 1, near - TY :] = high
            z_sum(hop, way).start()

    local_products(4)
    local_products(6)
    z_hop(0)
    local_products(0)
    exchange(NY - 1, y1(0))
    z_hop(1)
    local_products(2)
    exchange(NY - 1, y1(1))
    arrived(NY - 1, gram_y)
    gsum[...] = (gy[0] + gy[1]) + (gy[2] + gy[3])

    def rows16(ref, index):
        return ref.at[:, pl.ds(pl.multiple_of(index * 16, 16), 16), :]

    def gram_z(d):
        return remote(rows16(gsum, (z + d) % NZ), gz.at[z], gz_s.at[d - 1], gz_r.at[d - 1], at_z(d))

    exchange(NZ - 1, gram_z)
    gz[z] = gsum[:, pl.ds(pl.multiple_of(z * 16, 16), 16), :]
    z_hop(2)
    arrived(NZ - 1, gram_z)

    def gram_piece():
        return gram.at[x, pl.ds(2 * core, 2), pl.ds(pl.multiple_of(z * 16, 16), 16), :]

    total = gz[0]
    for i in range(1, NZ):
        total = total + gz[i]
    gram[x, pl.ds(2 * core, 2), pl.ds(pl.multiple_of(z * 16, 16), 16), :] = total

    def gram_all(d):
        return remote(gram_piece(), gram_piece(), ga_s.at[d - 1], ga_r.at[d - 1], at_z(d))

    exchange(NZ - 1, gram_all)
    z_hop(3)
    arrived(NZ - 1, gram_all)

    def gram_block(index):
        return gram.at[index, pl.ds(2 * core, 2), :, :]

    def gram_x(d):
        return remote(gram_block(x), gram_block(x), gx_s.at[d - 1], gx_r.at[d - 1], at_x(d))

    def gram_core(d):
        index = (x + NX - d) % NX
        return remote(gram_block(index), gram_block(index), gc_s.at[d], gc_r.at[d], other)

    exchange(NX - 1, gram_x)
    gram_core(0).start()

    def pass_on(d):
        gram_x(d).wait_recv()
        gram_core(d).start()

    for pair in range(TY // 2):
        arrived(NY - 1, y1(pair))
    sy[...] = (gl[0:TY, pl.ds(pl.multiple_of(y * 128, 128), 128), :] + ry[0]) + (ry[1] + ry[2])

    def z2(d):
        return remote(rows_of(sy, 0, TY, (z + d) % NZ, 16), rz2.at[d - 1], z2_s.at[d - 1], z2_r.at[d - 1], at_z(d))

    exchange(NZ - 1, z2)
    for way in range(2):
        z_sum(3, way).wait_recv()
    sz[...] = block(TY, TILES, z) + (in_r[2] + in_l[2])

    def y2(d):
        return remote(rows_of(sz, 0, TILES - TY, (y + d) % NY, 16), ry2.at[d - 1], y2_s.at[d - 1], y2_r.at[d - 1], at_y(d))

    exchange(NY - 1, y2)
    each(NX - 1, pass_on)

    for d in range(NX):
        gram_core(d).wait_recv()
    for k in range(4):
        for t in range(4):
            mm[B * k : B * (k + 1), B * t : B * (t + 1)] = gram[k, t] if t >= k else jnp.zeros((B, B), F32)
    factor_step(0, mm, dd)

    arrived(NZ - 1, z2)
    total = sy[:, pl.ds(pl.multiple_of(z * 16, 16), 16), :]
    for i in range(NZ - 1):
        total = total + rz2[i]
    gf[0:TY, pl.ds(pl.multiple_of((y * NZ + z) * 16, 16), 16), :] = total

    def z3(d):
        piece = rows_of(gf, 0, TY, y * NZ + z, 16)
        return remote(piece, piece, z3_s.at[d - 1], z3_r.at[d - 1], at_z(d))

    exchange(NZ - 1, z3)
    arrived(NY - 1, y2)
    total = sz[:, pl.ds(pl.multiple_of(y * 16, 16), 16), :]
    for i in range(NY - 1):
        total = total + ry2[i]
    gf[TY:TILES, pl.ds(pl.multiple_of((z * NY + y) * 16, 16), 16), :] = total

    def y3(d):
        piece = rows_of(gf, TY, TILES, z * NY + y, 16)
        return remote(piece, piece, y3_s.at[d - 1], y3_r.at[d - 1], at_y(d))

    exchange(NY - 1, y3)

    def y4(d):
        piece = rows_of(gf, 0, TY, y, 128)
        return remote(piece, piece, y4_s.at[d - 1], y4_r.at[d - 1], at_y(d))

    def z_all(hop, way):
        to = ways[way][0]
        index = (z + NZ - hop) % NZ if way == 0 else (z + hop) % NZ
        lo, hi = TY, TILES
        if hop == 3:
            lo, hi = (TY, near) if way == 0 else (near, TILES)
        piece = rows_of(gf, lo, hi, index, 64)
        return remote(piece, piece, all_s.at[way, hop], all_r.at[way, hop], at_z(to))

    def hop(number):
        for way in range(2):
            if number:
                z_all(number - 1, way).wait_recv()
            z_all(number, way).start()

    def begin():
        arrived(NY - 1, y3)
        hop(0)

    factor_step(1, mm, dd, begin)
    arrived(NZ - 1, z3)
    exchange(NY - 1, y4)
    hop(1)
    factor_step(2, mm, dd, lambda: hop(2))
    hop(3)
    factor_step(3, mm, dd)
    arrived(NY - 1, y4)
    for way in range(2):
        z_all(3, way).wait_recv()

    outs = [
        pltpu.make_async_copy(src, dst, out_sem.at[i])
        for i, (src, dst) in enumerate([(pt, p_hbm), (mm, m_hbm), (gf, g_hbm)])
    ]
    for copy in outs:
        copy.start()

    @pl.when(x == 0)
    def _():
        loop(half, lambda i: ring(i, 1).wait_send())
        loop(half, lambda i: ring(half + i, 1).wait_send())

    @pl.when(x == 1)
    def _():
        loop(half, lambda i: ring(i, 1).wait_send())

    @pl.when(x == 2)
    def _():
        loop(half, lambda i: ring(i, 1).wait_send())
        loop(half, lambda i: ring(half + i, 1).wait_send())

    @pl.when(x == 3)
    def _():
        loop(half, lambda i: ring(half + i, 1).wait_send())

    loop(NCH, lambda i: across(i).wait_send())
    for count, make in (
        (NY - 1, gram_y), (NZ - 1, gram_z), (NZ - 1, gram_all), (NX - 1, gram_x),
        (NY - 1, y1(0)), (NY - 1, y1(1)), (NZ - 1, z2), (NY - 1, y2), (NZ - 1, z3), (NY - 1, y3), (NY - 1, y4),
    ):
        sent(count, make)
    for d in range(NX):
        gram_core(d).wait_send()
    for way in range(2):
        for number in range(4):
            z_sum(number, way).wait_send()
            z_all(number, way).wait_send()
    for copy in outs:
        copy.wait()


def gather_products(flat):
    dma = pltpu.SemaphoreType.DMA
    tz = TILES - TY
    y_pair = [dma((NY - 1,)), dma((NY - 1,))]
    z_pair = [dma((NZ - 1,)), dma((NZ - 1,))]
    x_pair = [dma((NX - 1,)), dma((NX - 1,))]
    any_space = pl.BlockSpec(memory_space=pl.ANY)
    return pl.pallas_call(
        gather_kernel,
        out_shape=(
            jax.ShapeDtypeStruct((4, ROWS, B), F32),
            jax.ShapeDtypeStruct((WIDTH, WIDTH), F32),
            jax.ShapeDtypeStruct((TILES, WIDTH, B), F32),
        ),
        in_specs=[any_space],
        out_specs=(any_space,) * 3,
        scratch_shapes=[
            pltpu.VMEM((ROWS * TILES, B), F32),
            pltpu.VMEM((4, ROWS, B), F32),
            pltpu.VMEM((WIDTH, ROWS), BF16),
            pltpu.VMEM((WIDTH, ROWS), BF16),
            pltpu.VMEM((WIDTH, WIDTH), F32),
            pltpu.VMEM((B, B), F32),
            pltpu.VMEM((2, B, B), F32),
            pltpu.VMEM((NY, 2, B, B), F32),
            pltpu.VMEM((2, B, B), F32),
            pltpu.VMEM((NZ, 2, 16, B), F32),
            pltpu.VMEM((4, 4, B, B), F32),
            pltpu.VMEM((TILES, WIDTH, B), F32),
            pltpu.VMEM((TILES, WIDTH, B), F32),
            pltpu.VMEM((NY - 1, TY, 128, B), F32),
            pltpu.VMEM((TY, 128, B), F32),
            pltpu.VMEM((NZ - 1, TY, 16, B), F32),
            pltpu.VMEM((2, tz // 2, 64, B), F32),
            *[pltpu.VMEM((3, tz, 64, B), F32)] * 4,
            pltpu.VMEM((tz, 64, B), F32),
            pltpu.VMEM((NY - 1, tz, 16, B), F32),
            dma((NCH,)),
            dma((NCH,)), dma((NCH,)), dma((NCH,)), dma((NCH,)),
            *y_pair, *z_pair, *z_pair, *x_pair, dma((NX,)), dma((NX,)),
            dma((TY // 2, NY - 1)), dma((TY // 2, NY - 1)), dma((2, 4)), dma((2, 4)),
            *z_pair, *y_pair, *z_pair, *y_pair, *y_pair, dma((2, 4)), dma((2, 4)),
            dma((3,)),
        ],
        compiler_params=pltpu.CompilerParams(
            collective_id=0, has_side_effects=True, vmem_limit_bytes=48 << 20
        ),
        name="gather_products",
    )(flat)


def project_kernel(a_ref, p_ref, m_ref, g_ref, rows_ref, basis_ref, trail_ref, wh, wl):
    rows = p_ref.shape[1]
    inverse = split(m_ref[...])
    half = WIDTH // 2

    @pl.when(pl.program_id(0) == 0)
    def _():
        for t in range(0, TILES, 2):
            g = split(jnp.concatenate([g_ref[t], g_ref[t + 1]], axis=1))
            upper = dot3([v[:half, :half] for v in inverse], [v[:half] for v in g], ((1,), (0,)))
            lower = dot3([v[half:] for v in inverse], g, ((1,), (0,)))
            w = jnp.concatenate([upper, lower], axis=0)
            for h in range(2):
                rows_ref[pl.ds(t + h, WIDTH, stride=TILES), :] = w[:, B * h : B * (h + 1)]
            wh[t // 2], wl[t // 2] = split(w)

    panel = split(jnp.concatenate([p_ref[q] for q in range(4)], axis=1))
    basis = dot3(panel, inverse, ((1,), (1,)))
    for q in range(4):
        basis_ref[pl.ds((q % 2) * 2 + q // 2, rows, stride=4), :] = basis[:, B * q : B * (q + 1)]
    pair = split(basis)
    for t in range(0, TILES, 2):
        part = dot3(pair, (wh[t // 2], wl[t // 2]), ((1,), (0,)))
        for h in range(2):
            spot = pl.ds(t + h, rows, stride=TILES)
            trail_ref[spot, :] = a_ref[spot, :] - part[:, B * h : B * (h + 1)]


def project(flat, panels, inverse, products):
    steps = 4
    rows = ROWS // steps
    return pl.pallas_call(
        project_kernel,
        grid=(steps,),
        out_shape=(
            jax.ShapeDtypeStruct((WIDTH * TILES, B), F32),
            jax.ShapeDtypeStruct((ROWS * 4, B), F32),
            jax.ShapeDtypeStruct((ROWS * TILES, B), F32),
        ),
        in_specs=[
            pl.BlockSpec((rows * TILES, B), lambda i: (i, 0)),
            pl.BlockSpec((4, rows, B), lambda i: (0, i, 0)),
            pl.BlockSpec((WIDTH, WIDTH), lambda i: (0, 0)),
            pl.BlockSpec((TILES, WIDTH, B), lambda i: (0, 0, 0)),
        ],
        out_specs=(
            pl.BlockSpec((WIDTH * TILES, B), lambda i: (0, 0)),
            pl.BlockSpec((rows * 4, B), lambda i: (i, 0)),
            pl.BlockSpec((rows * TILES, B), lambda i: (i, 0)),
        ),
        scratch_shapes=[pltpu.VMEM((TILES // 2, WIDTH, 2 * B), BF16)] * 2,
        compiler_params=pltpu.CompilerParams(vmem_limit_bytes=40 << 20),
        name="project",
    )(flat, panels, inverse, products)


def on_device(features):
    flat = features.reshape(ROWS * TILES, B)
    panels, inverse, products = gather_products(flat)
    factor_rows, basis, trailing = project(flat, panels, inverse, products)
    basis = basis.reshape(ROWS, 2, 2, B).transpose(0, 2, 1, 3).reshape(ROWS, 2, 256)
    return (factor_rows.reshape(WIDTH, 4, 1, 256), basis, trailing.reshape(features.shape))


def solution(mesh):
    placed = (P("rows", None, "cols", None),)
    return jax.shard_map(
        on_device,
        mesh=mesh,
        in_specs=placed,
        out_specs=(
            P(None, None, "cols", None),
            P("rows", None, None),
            P("rows", None, "cols", None),
        ),
        check_vma=False,
    )
```

```python
import jax
import jax.numpy as jnp
from jax import lax
from jax.experimental import pallas as pl
from jax.experimental.pallas import tpu as pltpu
from jax.sharding import PartitionSpec as P

HIGHEST = lax.Precision.HIGHEST
F32 = jnp.float32
BF16 = jnp.bfloat16
MESH = pl.DeviceIdType.MESH

NY = 4
NZ = 8
NX = 4
ROWS = 1024
WIDTH = 512
B = 128
GR = 8
TILES = 8
TY = 4
CH = 64
NCH = ROWS // CH


def dot(a, b, dims):
    return lax.dot_general(a, b, (dims, ((), ())), precision=HIGHEST, preferred_element_type=F32)


def split(value):
    high = value.astype(BF16)
    return high, (value - high.astype(F32)).astype(BF16)


def dot3(a, b, dims):
    def one(u, v):
        return lax.dot_general(u, v, (dims, ((), ())), preferred_element_type=F32)

    return one(a[0], b[0]) + (one(a[0], b[1]) + one(a[1], b[0]))

def rows_bcast(x, j):
    return jnp.broadcast_to(x[j:j + 1, :], x.shape)

def lane_bcast(x, c):
    return jnp.broadcast_to(x[:, c:c + 1], x.shape)

def leaf(x_ref, hooks):
    n = B // GR
    lane = lax.broadcasted_iota(jnp.int32, (GR, B), 1)
    sub = lax.broadcasted_iota(jnp.int32, (GR, B), 0)
    x = [x_ref[GR * t:GR * (t + 1), :] for t in range(n)]
    for g in range(n):
        if g in hooks:
            hooks[g]()
        base = GR * g
        cur = x[g]
        v = [lane_bcast(cur, base + c) for c in range(GR)]
        in_group = (lane >= base) & (lane < base + GR)
        scale, mult, rows = [], {}, []
        for j in range(GR):
            r = lax.rsqrt(rows_bcast(v[j], j))
            w = jnp.where(sub > j, v[j] * r, 0.0)
            row = jnp.where(lane == base + j, r, rows_bcast(cur, j) * r)
            cur = jnp.where(sub == j, row, jnp.where((lane == base + j) & (sub > j), 0.0, cur) - w * row)
            for c in range(j + 1, GR):
                m = rows_bcast(v[c], j) * r
                mult[j, c] = m
                v[c] = v[c] - w * m
            scale.append(r)
            rows.append(jnp.where(in_group & (lane > base + j), 0.0, row))
        x[g] = cur
        for t in range(g + 1, n):
            xt = x[t]
            u = [lane_bcast(xt, base + c) for c in range(GR)]
            xt = jnp.where(in_group, 0.0, xt)
            for j in range(GR):
                w = u[j] * scale[j]
                for c in range(j + 1, GR):
                    u[c] = u[c] - w * mult[j, c]
                xt = xt - w * rows[j]
            x[t] = xt
    for t in range(n):
        x_ref[GR * t:GR * (t + 1), :] = x[t]

def factor_step(k, m_ref, d_ref, hooks):
    size = m_ref.shape[0]
    sl = slice(B * k, B * (k + 1))
    d_ref[...] = m_ref[sl, sl]
    leaf(d_ref, hooks)
    ri = lax.broadcasted_iota(jnp.int32, (B, B), 0)
    ci = lax.broadcasted_iota(jnp.int32, (B, B), 1)
    m = jnp.where(ri >= ci, d_ref[...], 0.0)
    m_ref[sl, sl] = m
    if k:
        left = dot(m, m_ref[sl, : B * k], ((1,), (0,)))
        m_ref[sl, : B * k] = left
    if B * (k + 1) < size:
        rest = slice(B * (k + 1), size)
        up = dot(m, m_ref[sl, rest], ((1,), (0,)))
        m_ref[sl, rest] = jnp.zeros_like(up)
        m_ref[rest, rest] = m_ref[rest, rest] - dot(up, up, ((0,), (0,)))
        m_ref[rest, sl] = -dot(up, m, ((0,), (0,)))
        if k:
            m_ref[rest, : B * k] = m_ref[rest, : B * k] - dot(up, left, ((0,), (0,)))


def each(count, body):
    def step(i, carry):
        body(i + 1)
        return carry

    lax.fori_loop(0, count, step, 0)


def exchange(count, make):
    each(count, lambda d: make(d).start())


def arrived(count, make):
    each(count, lambda d: make(d).wait_recv())


def sent(count, make):
    each(count, lambda d: make(d).wait_send())


def gather_kernel(
    a_hbm, p_hbm, m_hbm, g_hbm,
    av, pt, ph, pl_, mm, dd, gs, gy, gsum, gz, gram, gl, gf, ry, sy, rz2, first_in, in_r, in_l, out_r, out_l, sz, ry2,
    load_sem, ring_s, ring_r, core_s, core_r, gy_s, gy_r, gz_s, gz_r, ga_s, ga_r, gx_s, gx_r, gc_s, gc_r,
    y1_s, y1_r, sum_s, sum_r, z2_s, z2_r, y2_s, y2_r, z3_s, z3_r, y3_s, y3_r, y4_s, y4_r, all_s, all_r, out_sem,
):
    row = lax.axis_index("rows")
    col = lax.axis_index("cols")
    y, z = row % NY, row // NY
    x, core = col // 2, col % 2

    def at_y(d):
        return (z * NY + (y + d) % NY, col)

    def at_z(d):
        return (((z + d) % NZ) * NY + y, col)

    def at_x(d):
        return (row, ((x + d) % NX) * 2 + core)

    other = (row, x * 2 + 1 - core)

    def remote(src, dst, send, recv, device):
        return pltpu.make_async_remote_copy(
            src_ref=src, dst_ref=dst, send_sem=send, recv_sem=recv, device_id=device, device_id_type=MESH
        )

    def load(i):
        part = pl.ds(i * CH * TILES, CH * TILES)
        return pltpu.make_async_copy(a_hbm.at[part, :], av.at[part, :], load_sem.at[i])

    half = NCH // 2
    for i in range(half):
        load(i).start()
        load(half + i).start()

    barrier = pltpu.get_barrier_semaphore()

    def greet(device):
        pl.semaphore_signal(barrier, inc=1, device_id=device, device_id_type=MESH)

    each(NY - 1, lambda d: greet(at_y(d)))
    each(NZ - 1, lambda d: greet(at_z(d)))
    each(NX - 1, lambda d: greet(at_x(d)))
    greet(other)
    pl.semaphore_wait(barrier, (NY - 1) + (NZ - 1) + (NX - 1) + 1)

    def chunk(i):
        return pt.at[pl.ds(2 * core, 2), pl.ds(pl.multiple_of(i * CH, CH), CH), :]

    def ring(i, d):
        return remote(chunk(i), chunk(i), ring_s.at[i], ring_r.at[i], at_x(d))

    def across(i):
        return remote(chunk(i), chunk(i), core_s.at[i], core_r.at[i], other)

    def loop(count, body):
        def step(i, carry):
            body(i)
            return carry

        lax.fori_loop(0, count, step, 0)

    @pl.when(x == 0)
    def _():
        for i in range(half):
            for j in (i, half + i):
                load(j).wait()
                for h in range(2):
                    pt[2 * core + h, CH * j : CH * (j + 1), :] = av[pl.ds(CH * TILES * j + h, CH, stride=TILES), :]
            ring(i, 1).start()
            ring(half + i, NX - 1).start()
            across(i).start()
            across(half + i).start()

    @pl.when(x > 0)
    def _():
        for i in range(NCH):
            load(i).wait()

    @pl.when(x == 1)
    def _():
        def first(i):
            ring(i, 1).wait_recv()
            ring(i, 1).start()
            across(i).start()

        def second(i):
            ring(half + i, 1).wait_recv()
            across(half + i).start()

        loop(half, first)
        loop(half, second)

    @pl.when(x == 2)
    def _():
        def both(i):
            ring(i, 1).wait_recv()
            ring(i, 1).start()
            across(i).start()
            ring(half + i, 1).wait_recv()
            ring(half + i, NX - 1).start()
            across(half + i).start()

        loop(half, both)

    @pl.when(x == 3)
    def _():
        def first(i):
            ring(half + i, 1).wait_recv()
            ring(half + i, NX - 1).start()
            across(half + i).start()

        def second(i):
            ring(i, 1).wait_recv()
            across(i).start()

        loop(half, first)
        loop(half, second)

    loop(NCH, lambda i: across(i).wait_recv())

    left = pt[x]
    for h in range(2):
        gs[h] = dot(left, pt[2 * core + h], ((0,), (0,)))

    def rows16(ref, index):
        return ref.at[:, pl.ds(pl.multiple_of(index * 16, 16), 16), :]

    def gram_z(d):
        return remote(rows16(gs, (z + d) % NZ), gz.at[z], gz_s.at[d - 1], gz_r.at[d - 1], at_z(d))

    exchange(NZ - 1, gram_z)
    gz[z] = gs[:, pl.ds(pl.multiple_of(z * 16, 16), 16), :]

    for q in range(4):
        high, low = split(pt[q])
        ph[B * q : B * (q + 1), :] = high.T
        pl_[B * q : B * (q + 1), :] = low.T

    def local_products(t):
        tiles = [av[pl.ds(t + h, ROWS, stride=TILES), :] for h in range(2)]
        out = dot3((ph[...], pl_[...]), split(jnp.concatenate(tiles, axis=1)), ((1,), (0,)))
        gl[t] = out[:, :B]
        gl[t + 1] = out[:, B:]

    def rows_of(ref, lo, hi, index, size):
        return ref.at[lo:hi, pl.ds(pl.multiple_of(index * size, size), size), :]

    def y1(pair):
        lo = 2 * pair

        def make(d):
            src = rows_of(gl, lo, lo + 2, (y + d) % NY, 128)
            return remote(src, ry.at[d - 1, lo : lo + 2], y1_s.at[pair, d - 1], y1_r.at[pair, d - 1], at_y(d))

        return make

    ways = ((1, in_r, out_r), (NZ - 1, in_l, out_l))
    near = TY + (TILES - TY) // 2

    def block(lo, hi, index):
        return gl[lo:hi, pl.ds(pl.multiple_of((index % NZ) * 64, 64), 64), :]

    def z_sum(hop, way):
        to, into, out = ways[way]
        if hop == 0:
            lo, hi = (TY, near) if way == 0 else (near, TILES)
            src, dst = rows_of(gl, lo, hi, (z + 4) % NZ, 64), first_in.at[way]
        else:
            src, dst = out.at[hop - 1], into.at[hop - 1]
        return remote(src, dst, sum_s.at[way, hop], sum_r.at[way, hop], at_z(to))

    def z_hop(hop):
        for way, (to, into, out) in enumerate(ways):
            if hop > 0:
                z_sum(hop - 1, way).wait_recv()
                index = z + (4 - hop) if way == 0 else z + NZ - (4 - hop)
                low, high = block(TY, near, index), block(near, TILES, index)
                if hop == 1:
                    low, high = (low + first_in[0], high) if way == 0 else (low, high + first_in[1])
                else:
                    cut = near - TY
                    low, high = low + into[hop - 2, :cut], high + into[hop - 2, cut:]
                out[hop - 1, : near - TY] = low
                out[hop - 1, near - TY :] = high
            z_sum(hop, way).start()

    local_products(4)
    local_products(6)
    z_hop(0)
    local_products(0)
    exchange(NY - 1, y1(0))

    def z2(pair):
        lo = 2 * pair

        def make(d):
            src = rows_of(sy, lo, lo + 2, (z + d) % NZ, 16)
            return remote(src, rz2.at[d - 1, lo : lo + 2], z2_s.at[pair, d - 1], z2_r.at[pair, d - 1], at_z(d))

        return make

    def add_y(pair):
        part = slice(2 * pair, 2 * pair + 2)
        arrived(NY - 1, y1(pair))
        own = gl[part, pl.ds(pl.multiple_of(y * 128, 128), 128), :]
        sy[part] = (own + ry[0, part]) + (ry[1, part] + ry[2, part])
        exchange(NZ - 1, z2(pair))

    arrived(NZ - 1, gram_z)
    total = gz[0]
    for i in range(1, NZ):
        total = total + gz[i]
    gsum[...] = total

    def gram_y(d):
        return remote(gsum, gy.at[y], gy_s.at[d - 1], gy_r.at[d - 1], at_y(d))

    exchange(NY - 1, gram_y)
    gy[y] = gsum[...]
    z_hop(1)
    local_products(2)
    exchange(NY - 1, y1(1))
    arrived(NY - 1, gram_y)

    def gram_piece():
        return gram.at[x, pl.ds(2 * core, 2), pl.ds(pl.multiple_of(z * 16, 16), 16), :]

    gram[x, pl.ds(2 * core, 2), pl.ds(pl.multiple_of(z * 16, 16), 16), :] = (gy[0] + gy[1]) + (gy[2] + gy[3])

    def gram_all(d):
        return remote(gram_piece(), gram_piece(), ga_s.at[d - 1], ga_r.at[d - 1], at_z(d))

    exchange(NZ - 1, gram_all)
    z_hop(2)
    add_y(0)
    arrived(NZ - 1, gram_all)

    def gram_block(index):
        return gram.at[index, pl.ds(2 * core, 2), :, :]

    def gram_x(d):
        return remote(gram_block(x), gram_block(x), gx_s.at[d - 1], gx_r.at[d - 1], at_x(d))

    def gram_core(d):
        index = (x + NX - d) % NX
        return remote(gram_block(index), gram_block(index), gc_s.at[d], gc_r.at[d], other)

    exchange(NX - 1, gram_x)
    gram_core(0).start()

    def pass_on(d):
        gram_x(d).wait_recv()
        gram_core(d).start()

    z_hop(3)
    add_y(1)
    for way in range(2):
        z_sum(3, way).wait_recv()
    sz[...] = block(TY, TILES, z) + (in_r[2] + in_l[2])

    def y2(d):
        return remote(rows_of(sz, 0, TILES - TY, (y + d) % NY, 16), ry2.at[d - 1], y2_s.at[d - 1], y2_r.at[d - 1], at_y(d))

    exchange(NY - 1, y2)
    each(NX - 1, pass_on)

    for d in range(NX):
        gram_core(d).wait_recv()
    for k in range(4):
        for t in range(4):
            mm[B * k : B * (k + 1), B * t : B * (t + 1)] = gram[k, t] if t >= k else jnp.zeros((B, B), F32)
    def y3(d):
        piece = rows_of(gf, TY, TILES, z * NY + y, 16)
        return remote(piece, piece, y3_s.at[d - 1], y3_r.at[d - 1], at_y(d))

    arrived(NY - 1, y2)
    total = sz[:, pl.ds(pl.multiple_of(y * 16, 16), 16), :]
    for i in range(NY - 1):
        total = total + ry2[i]
    gf[TY:TILES, pl.ds(pl.multiple_of((z * NY + y) * 16, 16), 16), :] = total
    exchange(NY - 1, y3)

    def z3(d):
        piece = rows_of(gf, 0, TY, y * NZ + z, 16)
        return remote(piece, piece, z3_s.at[d - 1], z3_r.at[d - 1], at_z(d))

    def y4(source):
        piece = rows_of(gf, 0, TY, y * NZ + (z + NZ - source) % NZ, 16)

        def make(d):
            return remote(piece, piece, y4_s.at[source, d - 1], y4_r.at[source, d - 1], at_y(d))

        return make

    for pair in range(TY // 2):
        arrived(NZ - 1, z2(pair))
    total = sy[:, pl.ds(pl.multiple_of(z * 16, 16), 16), :]
    for i in range(NZ - 1):
        total = total + rz2[i]
    gf[0:TY, pl.ds(pl.multiple_of((y * NZ + z) * 16, 16), 16), :] = total
    exchange(NZ - 1, z3)
    exchange(NY - 1, y4(0))

    def z_all(hop, way):
        to = ways[way][0]
        index = (z + NZ - hop) % NZ if way == 0 else (z + hop) % NZ
        lo, hi = TY, TILES
        if hop == 3:
            lo, hi = (TY, near) if way == 0 else (near, TILES)
        piece = rows_of(gf, lo, hi, index, 64)
        return remote(piece, piece, all_s.at[way, hop], all_r.at[way, hop], at_z(to))

    def hop(number):
        for way in range(2):
            if number:
                z_all(number - 1, way).wait_recv()
            z_all(number, way).start()

    def begin():
        arrived(NY - 1, y3)
        hop(0)

    def forward(d):
        z3(d).wait_recv()
        exchange(NY - 1, y4(d))

    factor_step(0, mm, dd, {4: begin, 13: lambda: each(NZ - 1, forward)})
    factor_step(1, mm, dd, {3: lambda: hop(1)})
    factor_step(2, mm, dd, {2: lambda: hop(2)})
    factor_step(3, mm, dd, {1: lambda: hop(3)})
    loop(NZ, lambda source: arrived(NY - 1, y4(source)))
    for way in range(2):
        z_all(3, way).wait_recv()

    outs = [
        pltpu.make_async_copy(src, dst, out_sem.at[i])
        for i, (src, dst) in enumerate([(pt, p_hbm), (mm, m_hbm), (gf, g_hbm)])
    ]
    for copy in outs:
        copy.start()

    @pl.when(x == 0)
    def _():
        loop(half, lambda i: ring(i, 1).wait_send())
        loop(half, lambda i: ring(half + i, 1).wait_send())

    @pl.when(x == 1)
    def _():
        loop(half, lambda i: ring(i, 1).wait_send())

    @pl.when(x == 2)
    def _():
        loop(half, lambda i: ring(i, 1).wait_send())
        loop(half, lambda i: ring(half + i, 1).wait_send())

    @pl.when(x == 3)
    def _():
        loop(half, lambda i: ring(half + i, 1).wait_send())

    loop(NCH, lambda i: across(i).wait_send())
    for count, make in (
        (NY - 1, gram_y), (NZ - 1, gram_z), (NZ - 1, gram_all), (NX - 1, gram_x),
        (NY - 1, y1(0)), (NY - 1, y1(1)), (NZ - 1, z2(0)), (NZ - 1, z2(1)), (NY - 1, y2), (NZ - 1, z3), (NY - 1, y3),
    ):
        sent(count, make)
    for d in range(NX):
        gram_core(d).wait_send()
    loop(NZ, lambda source: sent(NY - 1, y4(source)))
    for way in range(2):
        for number in range(4):
            z_sum(number, way).wait_send()
            z_all(number, way).wait_send()
    for copy in outs:
        copy.wait()


def gather_products(flat):
    dma = pltpu.SemaphoreType.DMA
    tz = TILES - TY
    y_pair = [dma((NY - 1,)), dma((NY - 1,))]
    z_pair = [dma((NZ - 1,)), dma((NZ - 1,))]
    x_pair = [dma((NX - 1,)), dma((NX - 1,))]
    any_space = pl.BlockSpec(memory_space=pl.ANY)
    return pl.pallas_call(
        gather_kernel,
        out_shape=(
            jax.ShapeDtypeStruct((4, ROWS, B), F32),
            jax.ShapeDtypeStruct((WIDTH, WIDTH), F32),
            jax.ShapeDtypeStruct((TILES, WIDTH, B), F32),
        ),
        in_specs=[any_space],
        out_specs=(any_space,) * 3,
        scratch_shapes=[
            pltpu.VMEM((ROWS * TILES, B), F32),
            pltpu.VMEM((4, ROWS, B), F32),
            pltpu.VMEM((WIDTH, ROWS), BF16),
            pltpu.VMEM((WIDTH, ROWS), BF16),
            pltpu.VMEM((WIDTH, WIDTH), F32),
            pltpu.VMEM((B, B), F32),
            pltpu.VMEM((2, B, B), F32),
            pltpu.VMEM((NY, 2, 16, B), F32),
            pltpu.VMEM((2, 16, B), F32),
            pltpu.VMEM((NZ, 2, 16, B), F32),
            pltpu.VMEM((4, 4, B, B), F32),
            pltpu.VMEM((TILES, WIDTH, B), F32),
            pltpu.VMEM((TILES, WIDTH, B), F32),
            pltpu.VMEM((NY - 1, TY, 128, B), F32),
            pltpu.VMEM((TY, 128, B), F32),
            pltpu.VMEM((NZ - 1, TY, 16, B), F32),
            pltpu.VMEM((2, tz // 2, 64, B), F32),
            *[pltpu.VMEM((3, tz, 64, B), F32)] * 4,
            pltpu.VMEM((tz, 64, B), F32),
            pltpu.VMEM((NY - 1, tz, 16, B), F32),
            dma((NCH,)),
            dma((NCH,)), dma((NCH,)), dma((NCH,)), dma((NCH,)),
            *y_pair, *z_pair, *z_pair, *x_pair, dma((NX,)), dma((NX,)),
            dma((TY // 2, NY - 1)), dma((TY // 2, NY - 1)), dma((2, 4)), dma((2, 4)),
            dma((TY // 2, NZ - 1)), dma((TY // 2, NZ - 1)), *y_pair, *z_pair, *y_pair, dma((NZ, NY - 1)), dma((NZ, NY - 1)),
            dma((2, 4)), dma((2, 4)),
            dma((3,)),
        ],
        compiler_params=pltpu.CompilerParams(
            collective_id=0, has_side_effects=True, vmem_limit_bytes=48 << 20
        ),
        name="gather_products",
    )(flat)


def project_kernel(a_ref, p_ref, m_ref, g_ref, rows_hbm, basis_hbm, trail_hbm, wh, wl, rows_out, basis_out, trail_out, sems):
    inverse = split(m_ref[...])
    half = WIDTH // 2
    steps = 4
    rows = ROWS // steps

    def store(src, dst, size, index, sem):
        part = pl.ds(size * index, size)
        return pltpu.make_async_copy(src.at[part, :], dst.at[part, :], sem)

    copies = []

    def send(*args):
        copies.append(store(*args, sems.at[len(copies)]))
        copies[-1].start()

    pairs = []
    for i in range(steps):
        panel = split(jnp.concatenate([p_ref[q, rows * i : rows * (i + 1), :] for q in range(4)], axis=1))
        basis = dot3(panel, inverse, ((1,), (1,)))
        for q in range(4):
            basis_out[pl.ds(4 * rows * i + (q % 2) * 2 + q // 2, rows, stride=4), :] = basis[:, B * q : B * (q + 1)]
        bh, bl = split(basis)
        pairs.append((bh, bl))
        send(basis_out, basis_hbm, 4 * rows, i)
    for t in range(0, TILES, 2):
        g = split(jnp.concatenate([g_ref[t], g_ref[t + 1]], axis=1))
        upper = dot3([v[:half, :half] for v in inverse], [v[:half] for v in g], ((1,), (0,)))
        lower = dot3([v[half:] for v in inverse], g, ((1,), (0,)))
        w = jnp.concatenate([upper, lower], axis=0)
        for h in range(2):
            rows_out[pl.ds(t + h, WIDTH, stride=TILES), :] = w[:, B * h : B * (h + 1)]
        wh[t // 2], wl[t // 2] = split(w)
    send(rows_out, rows_hbm, WIDTH * TILES, 0)
    for i in range(steps):
        for t in range(0, TILES, 2):
            part = dot3(pairs[i], (wh[t // 2], wl[t // 2]), ((1,), (0,)))
            for h in range(2):
                spot = pl.ds(TILES * rows * i + t + h, rows, stride=TILES)
                trail_out[spot, :] = a_ref[spot, :] - part[:, B * h : B * (h + 1)]
        send(trail_out, trail_hbm, TILES * rows, i)
    for copy in copies:
        copy.wait()


def project(flat, panels, inverse, products):
    any_space = pl.BlockSpec(memory_space=pl.ANY)
    shapes = ((WIDTH * TILES, B), (ROWS * 4, B), (ROWS * TILES, B))
    return pl.pallas_call(
        project_kernel,
        out_shape=tuple(jax.ShapeDtypeStruct(shape, F32) for shape in shapes),
        in_specs=[pl.BlockSpec(memory_space=pltpu.VMEM)] * 4,
        out_specs=(any_space,) * 3,
        scratch_shapes=[
            *[pltpu.VMEM((TILES // 2, WIDTH, 2 * B), BF16)] * 2,
            *[pltpu.VMEM(shape, F32) for shape in shapes],
            pltpu.SemaphoreType.DMA((9,)),
        ],
        compiler_params=pltpu.CompilerParams(vmem_limit_bytes=32 << 20),
        name="project",
    )(flat, panels, inverse, products)


def on_device(features):
    flat = features.reshape(ROWS * TILES, B)
    panels, inverse, products = gather_products(flat)
    factor_rows, basis, trailing = project(flat, panels, inverse, products)
    basis = basis.reshape(ROWS, 2, 2, B).transpose(0, 2, 1, 3).reshape(ROWS, 2, 256)
    return (factor_rows.reshape(WIDTH, 4, 1, 256), basis, trailing.reshape(features.shape))


def solution(mesh):
    placed = (P("rows", None, "cols", None),)
    return jax.shard_map(
        on_device,
        mesh=mesh,
        in_specs=placed,
        out_specs=(
            P(None, None, "cols", None),
            P("rows", None, None),
            P("rows", None, "cols", None),
        ),
        check_vma=False,
    )
```

```python
import jax
import jax.numpy as jnp
from jax import lax
from jax.experimental import pallas as pl
from jax.experimental.pallas import tpu as pltpu
from jax.sharding import PartitionSpec as P

HIGHEST = lax.Precision.HIGHEST
F32 = jnp.float32
BF16 = jnp.bfloat16
MESH = pl.DeviceIdType.MESH

NY = 4
NZ = 8
NX = 4
ROWS = 1024
WIDTH = 512
B = 128
GR = 8
TILES = 8
TY = 4
CH = 64
NCH = ROWS // CH


def dot(a, b, dims):
    return lax.dot_general(a, b, (dims, ((), ())), precision=HIGHEST, preferred_element_type=F32)


def split(value):
    high = value.astype(BF16)
    return high, (value - high.astype(F32)).astype(BF16)


def dot3(a, b, dims):
    def one(u, v):
        return lax.dot_general(u, v, (dims, ((), ())), preferred_element_type=F32)

    return one(a[0], b[0]) + (one(a[0], b[1]) + one(a[1], b[0]))

def rows_bcast(x, j):
    return jnp.broadcast_to(x[j:j + 1, :], x.shape)

def lane_bcast(x, c):
    return jnp.broadcast_to(x[:, c:c + 1], x.shape)

def leaf(x_ref, hooks):
    n = B // GR
    lane = lax.broadcasted_iota(jnp.int32, (GR, B), 1)
    sub = lax.broadcasted_iota(jnp.int32, (GR, B), 0)
    x = [x_ref[GR * t:GR * (t + 1), :] for t in range(n)]
    for g in range(n):
        if g in hooks:
            hooks[g]()
        base = GR * g
        cur = x[g]
        v = [lane_bcast(cur, base + c) for c in range(GR)]
        in_group = (lane >= base) & (lane < base + GR)
        scale, mult, rows = [], {}, []
        for j in range(GR):
            r = lax.rsqrt(rows_bcast(v[j], j))
            w = jnp.where(sub > j, v[j] * r, 0.0)
            row = jnp.where(lane == base + j, r, rows_bcast(cur, j) * r)
            cur = jnp.where(sub == j, row, jnp.where((lane == base + j) & (sub > j), 0.0, cur) - w * row)
            for c in range(j + 1, GR):
                m = rows_bcast(v[c], j) * r
                mult[j, c] = m
                v[c] = v[c] - w * m
            scale.append(r)
            rows.append(jnp.where(in_group & (lane > base + j), 0.0, row))
        x[g] = cur
        for t in range(g + 1, n):
            xt = x[t]
            u = [lane_bcast(xt, base + c) for c in range(GR)]
            xt = jnp.where(in_group, 0.0, xt)
            for j in range(GR):
                w = u[j] * scale[j]
                for c in range(j + 1, GR):
                    u[c] = u[c] - w * mult[j, c]
                xt = xt - w * rows[j]
            x[t] = xt
    for t in range(n):
        x_ref[GR * t:GR * (t + 1), :] = x[t]

def factor_step(k, m_ref, d_ref, hooks):
    size = m_ref.shape[0]
    sl = slice(B * k, B * (k + 1))
    d_ref[...] = m_ref[sl, sl]
    leaf(d_ref, hooks)
    ri = lax.broadcasted_iota(jnp.int32, (B, B), 0)
    ci = lax.broadcasted_iota(jnp.int32, (B, B), 1)
    m = jnp.where(ri >= ci, d_ref[...], 0.0)
    m_ref[sl, sl] = m
    if k:
        left = dot(m, m_ref[sl, : B * k], ((1,), (0,)))
        m_ref[sl, : B * k] = left
    if B * (k + 1) < size:
        rest = slice(B * (k + 1), size)
        up = dot(m, m_ref[sl, rest], ((1,), (0,)))
        m_ref[sl, rest] = jnp.zeros_like(up)
        m_ref[rest, rest] = m_ref[rest, rest] - dot(up, up, ((0,), (0,)))
        m_ref[rest, sl] = -dot(up, m, ((0,), (0,)))
        if k:
            m_ref[rest, : B * k] = m_ref[rest, : B * k] - dot(up, left, ((0,), (0,)))


def each(count, body):
    def step(i, carry):
        body(i + 1)
        return carry

    lax.fori_loop(0, count, step, 0)


def exchange(count, make):
    each(count, lambda d: make(d).start())


def arrived(count, make):
    each(count, lambda d: make(d).wait_recv())


def sent(count, make):
    each(count, lambda d: make(d).wait_send())


def gather_kernel(
    a_hbm, p_hbm, m_hbm, g_hbm,
    av, pt, ph, pl_, mm, dd, gs, gy, gsum, gz, gram, gl, gf, ry, sy, rz2, first_in, in_r, in_l, out_r, out_l, sz, ry2,
    load_sem, ring_s, ring_r, core_s, core_r, gy_s, gy_r, gz_s, gz_r, ga_s, ga_r, gx_s, gx_r, gc_s, gc_r,
    y1_s, y1_r, sum_s, sum_r, z2_s, z2_r, y2_s, y2_r, z3_s, z3_r, y3_s, y3_r, y4_s, y4_r, all_s, all_r, out_sem,
):
    row = lax.axis_index("rows")
    col = lax.axis_index("cols")
    y, z = row % NY, row // NY
    x, core = col // 2, col % 2

    def at_y(d):
        return (z * NY + (y + d) % NY, col)

    def at_z(d):
        return (((z + d) % NZ) * NY + y, col)

    def at_x(d):
        return (row, ((x + d) % NX) * 2 + core)

    other = (row, x * 2 + 1 - core)

    def remote(src, dst, send, recv, device):
        return pltpu.make_async_remote_copy(
            src_ref=src, dst_ref=dst, send_sem=send, recv_sem=recv, device_id=device, device_id_type=MESH
        )

    def load(i):
        part = pl.ds(i * CH * TILES, CH * TILES)
        return pltpu.make_async_copy(a_hbm.at[part, :], av.at[part, :], load_sem.at[i])

    half = NCH // 2
    for i in range(half):
        load(i).start()
        load(half + i).start()

    barrier = pltpu.get_barrier_semaphore()

    def greet(device):
        pl.semaphore_signal(barrier, inc=1, device_id=device, device_id_type=MESH)

    each(NY - 1, lambda d: greet(at_y(d)))
    each(NZ - 1, lambda d: greet(at_z(d)))
    each(NX - 1, lambda d: greet(at_x(d)))
    greet(other)
    pl.semaphore_wait(barrier, (NY - 1) + (NZ - 1) + (NX - 1) + 1)

    def chunk(i):
        return pt.at[pl.ds(2 * core, 2), pl.ds(pl.multiple_of(i * CH, CH), CH), :]

    def ring(i, d):
        return remote(chunk(i), chunk(i), ring_s.at[i], ring_r.at[i], at_x(d))

    def across(i):
        return remote(chunk(i), chunk(i), core_s.at[i], core_r.at[i], other)

    def loop(count, body):
        def step(i, carry):
            body(i)
            return carry

        lax.fori_loop(0, count, step, 0)

    @pl.when(x == 0)
    def _():
        for i in range(half):
            for j in (i, half + i):
                load(j).wait()
                for h in range(2):
                    pt[2 * core + h, CH * j : CH * (j + 1), :] = av[pl.ds(CH * TILES * j + h, CH, stride=TILES), :]
            ring(i, 1).start()
            ring(half + i, NX - 1).start()
            across(i).start()
            across(half + i).start()

    @pl.when(x > 0)
    def _():
        for i in range(NCH):
            load(i).wait()

    @pl.when(x == 1)
    def _():
        def first(i):
            ring(i, 1).wait_recv()
            ring(i, 1).start()
            across(i).start()

        def second(i):
            ring(half + i, 1).wait_recv()
            across(half + i).start()

        loop(half, first)
        loop(half, second)

    @pl.when(x == 2)
    def _():
        def both(i):
            ring(i, 1).wait_recv()
            ring(i, 1).start()
            across(i).start()
            ring(half + i, 1).wait_recv()
            ring(half + i, NX - 1).start()
            across(half + i).start()

        loop(half, both)

    @pl.when(x == 3)
    def _():
        def first(i):
            ring(half + i, 1).wait_recv()
            ring(half + i, NX - 1).start()
            across(half + i).start()

        def second(i):
            ring(i, 1).wait_recv()
            across(i).start()

        loop(half, first)
        loop(half, second)

    loop(NCH, lambda i: across(i).wait_recv())

    left = pt[x]
    for h in range(2):
        gs[h] = dot(left, pt[2 * core + h], ((0,), (0,)))

    def rows16(ref, index):
        return ref.at[:, pl.ds(pl.multiple_of(index * 16, 16), 16), :]

    def gram_z(d):
        return remote(rows16(gs, (z + d) % NZ), gz.at[z], gz_s.at[d - 1], gz_r.at[d - 1], at_z(d))

    exchange(NZ - 1, gram_z)
    gz[z] = gs[:, pl.ds(pl.multiple_of(z * 16, 16), 16), :]

    for q in range(4):
        high, low = split(pt[q])
        ph[B * q : B * (q + 1), :] = high.T
        pl_[B * q : B * (q + 1), :] = low.T

    def local_products(t):
        tiles = [av[pl.ds(t + h, ROWS, stride=TILES), :] for h in range(2)]
        out = dot3((ph[...], pl_[...]), split(jnp.concatenate(tiles, axis=1)), ((1,), (0,)))
        gl[t] = out[:, :B]
        gl[t + 1] = out[:, B:]

    def rows_of(ref, lo, hi, index, size):
        return ref.at[lo:hi, pl.ds(pl.multiple_of(index * size, size), size), :]

    def y1(pair):
        lo = 2 * pair

        def make(d):
            src = rows_of(gl, lo, lo + 2, (y + d) % NY, 128)
            return remote(src, ry.at[d - 1, lo : lo + 2], y1_s.at[pair, d - 1], y1_r.at[pair, d - 1], at_y(d))

        return make

    ways = ((1, in_r, out_r), (NZ - 1, in_l, out_l))
    near = TY + (TILES - TY) // 2

    def block(lo, hi, index):
        return gl[lo:hi, pl.ds(pl.multiple_of((index % NZ) * 64, 64), 64), :]

    def z_sum(hop, way):
        to, into, out = ways[way]
        if hop == 0:
            lo, hi = (TY, near) if way == 0 else (near, TILES)
            src, dst = rows_of(gl, lo, hi, (z + 4) % NZ, 64), first_in.at[way]
        else:
            src, dst = out.at[hop - 1], into.at[hop - 1]
        return remote(src, dst, sum_s.at[way, hop], sum_r.at[way, hop], at_z(to))

    def z_hop(hop):
        for way, (to, into, out) in enumerate(ways):
            if hop > 0:
                z_sum(hop - 1, way).wait_recv()
                index = z + (4 - hop) if way == 0 else z + NZ - (4 - hop)
                low, high = block(TY, near, index), block(near, TILES, index)
                if hop == 1:
                    low, high = (low + first_in[0], high) if way == 0 else (low, high + first_in[1])
                else:
                    cut = near - TY
                    low, high = low + into[hop - 2, :cut], high + into[hop - 2, cut:]
                out[hop - 1, : near - TY] = low
                out[hop - 1, near - TY :] = high
            z_sum(hop, way).start()

    local_products(4)
    local_products(6)
    z_hop(0)
    local_products(0)
    exchange(NY - 1, y1(0))

    def z2(pair):
        lo = 2 * pair

        def make(d):
            src = rows_of(sy, lo, lo + 2, (z + d) % NZ, 16)
            return remote(src, rz2.at[d - 1, lo : lo + 2], z2_s.at[pair, d - 1], z2_r.at[pair, d - 1], at_z(d))

        return make

    def add_y(pair):
        part = slice(2 * pair, 2 * pair + 2)
        arrived(NY - 1, y1(pair))
        own = gl[part, pl.ds(pl.multiple_of(y * 128, 128), 128), :]
        sy[part] = (own + ry[0, part]) + (ry[1, part] + ry[2, part])
        exchange(NZ - 1, z2(pair))

    arrived(NZ - 1, gram_z)
    total = gz[0]
    for i in range(1, NZ):
        total = total + gz[i]
    gsum[...] = total

    def gram_y(d):
        return remote(gsum, gy.at[y], gy_s.at[d - 1], gy_r.at[d - 1], at_y(d))

    exchange(NY - 1, gram_y)
    gy[y] = gsum[...]
    z_hop(1)
    local_products(2)
    exchange(NY - 1, y1(1))
    arrived(NY - 1, gram_y)

    def gram_piece():
        return gram.at[x, pl.ds(2 * core, 2), pl.ds(pl.multiple_of(z * 16, 16), 16), :]

    gram[x, pl.ds(2 * core, 2), pl.ds(pl.multiple_of(z * 16, 16), 16), :] = (gy[0] + gy[1]) + (gy[2] + gy[3])

    def gram_all(d):
        return remote(gram_piece(), gram_piece(), ga_s.at[d - 1], ga_r.at[d - 1], at_z(d))

    exchange(NZ - 1, gram_all)
    z_hop(2)
    add_y(0)
    arrived(NZ - 1, gram_all)

    def gram_block(index):
        return gram.at[index, pl.ds(2 * core, 2), :, :]

    def gram_x(d):
        return remote(gram_block(x), gram_block(x), gx_s.at[d - 1], gx_r.at[d - 1], at_x(d))

    def gram_core(d):
        index = (x + NX - d) % NX
        return remote(gram_block(index), gram_block(index), gc_s.at[d], gc_r.at[d], other)

    exchange(NX - 1, gram_x)
    gram_core(0).start()

    def pass_on(d):
        gram_x(d).wait_recv()
        gram_core(d).start()

    z_hop(3)
    add_y(1)
    for way in range(2):
        z_sum(3, way).wait_recv()
    sz[...] = block(TY, TILES, z) + (in_r[2] + in_l[2])

    def y2(d):
        return remote(rows_of(sz, 0, TILES - TY, (y + d) % NY, 16), ry2.at[d - 1], y2_s.at[d - 1], y2_r.at[d - 1], at_y(d))

    exchange(NY - 1, y2)
    each(NX - 1, pass_on)

    for d in range(NX):
        gram_core(d).wait_recv()
    for k in range(4):
        for t in range(4):
            mm[B * k : B * (k + 1), B * t : B * (t + 1)] = gram[k, t] if t >= k else jnp.zeros((B, B), F32)
    def y3(d):
        piece = rows_of(gf, TY, TILES, z * NY + y, 16)
        return remote(piece, piece, y3_s.at[d - 1], y3_r.at[d - 1], at_y(d))

    arrived(NY - 1, y2)
    total = sz[:, pl.ds(pl.multiple_of(y * 16, 16), 16), :]
    for i in range(NY - 1):
        total = total + ry2[i]
    gf[TY:TILES, pl.ds(pl.multiple_of((z * NY + y) * 16, 16), 16), :] = total
    exchange(NY - 1, y3)

    def z3(d):
        piece = rows_of(gf, 0, TY, y * NZ + z, 16)
        return remote(piece, piece, z3_s.at[d - 1], z3_r.at[d - 1], at_z(d))

    def y4(source):
        piece = rows_of(gf, 0, TY, y * NZ + (z + NZ - source) % NZ, 16)

        def make(d):
            return remote(piece, piece, y4_s.at[source, d - 1], y4_r.at[source, d - 1], at_y(d))

        return make

    for pair in range(TY // 2):
        arrived(NZ - 1, z2(pair))
    total = sy[:, pl.ds(pl.multiple_of(z * 16, 16), 16), :]
    for i in range(NZ - 1):
        total = total + rz2[i]
    gf[0:TY, pl.ds(pl.multiple_of((y * NZ + z) * 16, 16), 16), :] = total
    exchange(NZ - 1, z3)
    exchange(NY - 1, y4(0))

    def z_all(hop, way, part):
        to = ways[way][0]
        index = (z + NZ - hop) % NZ if way == 0 else (z + hop) % NZ
        lo, hi = (TY, near) if part == 0 else (near, TILES)
        piece = rows_of(gf, lo, hi, index, 64)
        return remote(piece, piece, all_s.at[way, hop, part], all_r.at[way, hop, part], at_z(to))

    legs = [(number, way, part) for number in range(4) for part in range(2) for way in range(2) if number < 3 or part == way]

    def hop(number):
        for leg in legs:
            if leg[0] == number:
                if number:
                    z_all(number - 1, *leg[1:]).wait_recv()
                z_all(*leg).start()

    def begin():
        arrived(NY - 1, y3)
        hop(0)

    def forward(d):
        z3(d).wait_recv()
        exchange(NY - 1, y4(d))

    factor_step(0, mm, dd, {4: begin, 13: lambda: each(NZ - 1, forward)})
    factor_step(1, mm, dd, {3: lambda: hop(1)})
    factor_step(2, mm, dd, {2: lambda: hop(2)})
    factor_step(3, mm, dd, {1: lambda: hop(3)})
    loop(NZ, lambda source: arrived(NY - 1, y4(source)))
    for number, way, part in legs:
        if number == 3 or (number == 2 and part != way):
            z_all(number, way, part).wait_recv()

    outs = [
        pltpu.make_async_copy(src, dst, out_sem.at[i])
        for i, (src, dst) in enumerate([(pt, p_hbm), (mm, m_hbm), (gf, g_hbm)])
    ]
    for copy in outs:
        copy.start()

    @pl.when(x == 0)
    def _():
        loop(half, lambda i: ring(i, 1).wait_send())
        loop(half, lambda i: ring(half + i, 1).wait_send())

    @pl.when(x == 1)
    def _():
        loop(half, lambda i: ring(i, 1).wait_send())

    @pl.when(x == 2)
    def _():
        loop(half, lambda i: ring(i, 1).wait_send())
        loop(half, lambda i: ring(half + i, 1).wait_send())

    @pl.when(x == 3)
    def _():
        loop(half, lambda i: ring(half + i, 1).wait_send())

    loop(NCH, lambda i: across(i).wait_send())
    for count, make in (
        (NY - 1, gram_y), (NZ - 1, gram_z), (NZ - 1, gram_all), (NX - 1, gram_x),
        (NY - 1, y1(0)), (NY - 1, y1(1)), (NZ - 1, z2(0)), (NZ - 1, z2(1)), (NY - 1, y2), (NZ - 1, z3), (NY - 1, y3),
    ):
        sent(count, make)
    for d in range(NX):
        gram_core(d).wait_send()
    loop(NZ, lambda source: sent(NY - 1, y4(source)))
    for way in range(2):
        for number in range(4):
            z_sum(number, way).wait_send()
    for leg in legs:
        z_all(*leg).wait_send()
    for copy in outs:
        copy.wait()


def gather_products(flat):
    dma = pltpu.SemaphoreType.DMA
    tz = TILES - TY
    y_pair = [dma((NY - 1,)), dma((NY - 1,))]
    z_pair = [dma((NZ - 1,)), dma((NZ - 1,))]
    x_pair = [dma((NX - 1,)), dma((NX - 1,))]
    any_space = pl.BlockSpec(memory_space=pl.ANY)
    return pl.pallas_call(
        gather_kernel,
        out_shape=(
            jax.ShapeDtypeStruct((4, ROWS, B), F32),
            jax.ShapeDtypeStruct((WIDTH, WIDTH), F32),
            jax.ShapeDtypeStruct((TILES, WIDTH, B), F32),
        ),
        in_specs=[any_space],
        out_specs=(any_space,) * 3,
        scratch_shapes=[
            pltpu.VMEM((ROWS * TILES, B), F32),
            pltpu.VMEM((4, ROWS, B), F32),
            pltpu.VMEM((WIDTH, ROWS), BF16),
            pltpu.VMEM((WIDTH, ROWS), BF16),
            pltpu.VMEM((WIDTH, WIDTH), F32),
            pltpu.VMEM((B, B), F32),
            pltpu.VMEM((2, B, B), F32),
            pltpu.VMEM((NY, 2, 16, B), F32),
            pltpu.VMEM((2, 16, B), F32),
            pltpu.VMEM((NZ, 2, 16, B), F32),
            pltpu.VMEM((4, 4, B, B), F32),
            pltpu.VMEM((TILES, WIDTH, B), F32),
            pltpu.VMEM((TILES, WIDTH, B), F32),
            pltpu.VMEM((NY - 1, TY, 128, B), F32),
            pltpu.VMEM((TY, 128, B), F32),
            pltpu.VMEM((NZ - 1, TY, 16, B), F32),
            pltpu.VMEM((2, tz // 2, 64, B), F32),
            *[pltpu.VMEM((3, tz, 64, B), F32)] * 4,
            pltpu.VMEM((tz, 64, B), F32),
            pltpu.VMEM((NY - 1, tz, 16, B), F32),
            dma((NCH,)),
            dma((NCH,)), dma((NCH,)), dma((NCH,)), dma((NCH,)),
            *y_pair, *z_pair, *z_pair, *x_pair, dma((NX,)), dma((NX,)),
            dma((TY // 2, NY - 1)), dma((TY // 2, NY - 1)), dma((2, 4)), dma((2, 4)),
            dma((TY // 2, NZ - 1)), dma((TY // 2, NZ - 1)), *y_pair, *z_pair, *y_pair, dma((NZ, NY - 1)), dma((NZ, NY - 1)),
            dma((2, 4, 2)), dma((2, 4, 2)),
            dma((3,)),
        ],
        compiler_params=pltpu.CompilerParams(
            collective_id=0, has_side_effects=True, vmem_limit_bytes=48 << 20
        ),
        name="gather_products",
    )(flat)


def project_kernel(a_ref, p_ref, m_ref, g_ref, rows_hbm, basis_hbm, trail_hbm, wh, wl, rows_out, basis_out, trail_out, sems):
    inverse = split(m_ref[...])
    half = WIDTH // 2
    steps = 4
    rows = ROWS // steps

    def store(src, dst, size, index, sem):
        part = pl.ds(size * index, size)
        return pltpu.make_async_copy(src.at[part, :], dst.at[part, :], sem)

    copies = []

    def send(*args):
        copies.append(store(*args, sems.at[len(copies)]))
        copies[-1].start()

    pairs = []
    for i in range(steps):
        panel = split(jnp.concatenate([p_ref[q, rows * i : rows * (i + 1), :] for q in range(4)], axis=1))
        basis = dot3(panel, inverse, ((1,), (1,)))
        for q in range(4):
            basis_out[pl.ds(4 * rows * i + (q % 2) * 2 + q // 2, rows, stride=4), :] = basis[:, B * q : B * (q + 1)]
        bh, bl = split(basis)
        pairs.append((bh, bl))
        send(basis_out, basis_hbm, 4 * rows, i)
    for t in range(0, TILES, 2):
        g = split(jnp.concatenate([g_ref[t], g_ref[t + 1]], axis=1))
        upper = dot3([v[:half, :half] for v in inverse], [v[:half] for v in g], ((1,), (0,)))
        lower = dot3([v[half:] for v in inverse], g, ((1,), (0,)))
        w = jnp.concatenate([upper, lower], axis=0)
        for h in range(2):
            rows_out[pl.ds(t + h, WIDTH, stride=TILES), :] = w[:, B * h : B * (h + 1)]
        wh[t // 2], wl[t // 2] = split(w)
    send(rows_out, rows_hbm, WIDTH * TILES, 0)
    for i in range(steps):
        for t in range(0, TILES, 2):
            part = dot3(pairs[i], (wh[t // 2], wl[t // 2]), ((1,), (0,)))
            for h in range(2):
                spot = pl.ds(TILES * rows * i + t + h, rows, stride=TILES)
                trail_out[spot, :] = a_ref[spot, :] - part[:, B * h : B * (h + 1)]
        send(trail_out, trail_hbm, TILES * rows, i)
    for copy in copies:
        copy.wait()


def project(flat, panels, inverse, products):
    any_space = pl.BlockSpec(memory_space=pl.ANY)
    shapes = ((WIDTH * TILES, B), (ROWS * 4, B), (ROWS * TILES, B))
    return pl.pallas_call(
        project_kernel,
        out_shape=tuple(jax.ShapeDtypeStruct(shape, F32) for shape in shapes),
        in_specs=[pl.BlockSpec(memory_space=pltpu.VMEM)] * 4,
        out_specs=(any_space,) * 3,
        scratch_shapes=[
            *[pltpu.VMEM((TILES // 2, WIDTH, 2 * B), BF16)] * 2,
            *[pltpu.VMEM(shape, F32) for shape in shapes],
            pltpu.SemaphoreType.DMA((9,)),
        ],
        compiler_params=pltpu.CompilerParams(vmem_limit_bytes=32 << 20),
        name="project",
    )(flat, panels, inverse, products)


def on_device(features):
    flat = features.reshape(ROWS * TILES, B)
    panels, inverse, products = gather_products(flat)
    factor_rows, basis, trailing = project(flat, panels, inverse, products)
    basis = basis.reshape(ROWS, 2, 2, B).transpose(0, 2, 1, 3).reshape(ROWS, 2, 256)
    return (factor_rows.reshape(WIDTH, 4, 1, 256), basis, trailing.reshape(features.shape))


def solution(mesh):
    placed = (P("rows", None, "cols", None),)
    return jax.shard_map(
        on_device,
        mesh=mesh,
        in_specs=placed,
        out_specs=(
            P(None, None, "cols", None),
            P("rows", None, None),
            P("rows", None, "cols", None),
        ),
        check_vma=False,
    )
```
